128 devices in a mesh: freq: 2 (over core), tile: 64 (over y, x, z).
Axes of the slice: x: 4, y: 4, z: 4, core: 2. Of those that a mesh axis runs over, the one named last changes fastest.
Arguments:
- wave_in: bfloat16 [2, 16384, 2, 256], P(None, 'tile', None, 'freq'), may hold values from -6 to 6
- column_basis: bfloat16 [2, 128, 64, 256, 128], P('freq', None, 'tile'), may hold values from -0.25 to 0.25
- row_basis: bfloat16 [2, 128, 64, 256, 128], P('freq', 'tile'), may hold values from -0.09375 to 0.09375
- tile_scale: float32 [2, 128, 64], P('freq'), may hold values from 0.5 to 2
- tile_ranks: int32 [2, 128, 64], P('freq'), may hold values from 16 to 64, as said below
Outputs:
- forward_out: bfloat16 [2, 32768, 2, 256], P('freq', 'tile')
- adjoint_out: bfloat16 [2, 16384, 2, 256], P(None, 'tile', None, 'freq')
The draws below stay inside these ranges and needn't reach their ends.
Inputs may be any that keep to these rules, and one draw needn't show every extreme that they name: `tile_ranks`: every entry is a multiple of 16. For each frequency, in each aligned group of 2 tile rows and 1 tile columns the ranks add up to at most 80, and some group reaches that sum.
All inputs are finite; a program needn't handle non-finite values.
Results may differ from the reference program's by a relative error of at most 0.005.
Values may be sent and summed in bfloat16 or wider, within the bound.
A program may use at most 192 MiB of HBM per device.

```python
import math
import jax
import jax.numpy as jnp
from jax import lax

NB = 256
RMAX = 64
MT_DEV = 2
NT_DEV = 1
NVS = 256
NF = 2
MT = 128
NT = 64
N = 16384
CAP = 5


def draw_tile_ranks(key, part):
    blocks_max = RMAX // 16
    group_rows = MT // MT_DEV
    group_cols = NT // NT_DEV
    key_total, key_split = jax.random.split(jax.random.fold_in(key, 7))
    extra_blocks = jax.random.randint(key_total, (NF, group_rows, group_cols), 0, CAP - 1)
    group_total = (extra_blocks + 2).at[0, 0, 0].set(CAP)
    lowest = jnp.maximum(1, group_total - blocks_max)
    highest = jnp.minimum(blocks_max, group_total - 1)
    spread = jax.random.randint(key_split, (NF, group_rows, group_cols), 0, 1048576)
    first_blocks = lowest + spread % (highest - lowest + 1)
    first_blocks = first_blocks.at[0, 0, 0].set(blocks_max)
    second = group_total - first_blocks
    paired = jnp.stack([first_blocks, second], -1).reshape(NF, group_rows, group_cols, MT_DEV, NT_DEV)
    paired = jnp.transpose(paired, (0, 1, 3, 2, 4)).reshape(NF, MT, NT)
    return (16 * paired).astype(jnp.int32)


def shard_levels(own_key, shape, shards, least, largest):
    level = 1.0
    for axis_at, parts in shards:
        steps = jax.random.uniform(jax.random.fold_in(jax.random.fold_in(own_key, 6), axis_at), (parts,), jnp.float32, least / len(shards), largest / len(shards))
        level = level * jnp.repeat(jnp.exp(steps), shape[axis_at] // parts).reshape((-1,) + (1,) * (len(shape) - 1 - axis_at))
    return level


def normal_values(rng, dims, scale, reach, cuts=(), kind=jnp.bfloat16):
    gain = shard_levels(rng, dims, cuts, -0.22, 0.18) if cuts else 1.0
    values = jax.random.normal(rng, dims, jnp.float32) * scale * gain
    return jnp.minimum(jnp.maximum(values, -reach), reach).astype(kind)


def setup_inputs(seed: int = 0) -> dict:
    seeds = jax.random.split(jax.random.key(seed), 6)
    wave_in = normal_values(seeds[0], (NF, N, 2, NVS), 1.0, 6.0, ((1, 64), (3, 2)))
    column_basis = normal_values(seeds[1], (NF, MT, NT, NB, 2 * RMAX), (2 * NB) ** -0.5, 0.25, ((0, 2), (2, 64)))
    row_basis = normal_values(seeds[2], (NF, MT, NT, NB, 2 * RMAX), (NT * RMAX) ** -0.5, 0.09375, ((0, 2), (1, 64)))
    tile_scale = jnp.clip(jnp.exp(math.log(2.0) - 1.3862944 * jax.random.uniform(seeds[3], (NF, MT, NT), jnp.float32) ** shard_levels(seeds[3], (NF, MT, NT), ((0, 2),), -0.2, 0.2)), 0.5, 2.0)
    tile_ranks = draw_tile_ranks(jax.random.fold_in(seeds[5], 71), 0)
    return {"wave_in": wave_in, "column_basis": column_basis, "row_basis": row_basis, "tile_scale": tile_scale, "tile_ranks": tile_ranks}


def combine_conj(products):
    shaped = products.reshape(products.shape[:-3] + (products.shape[-3] // 32, 2, 16) + products.shape[-2:])
    real_part = shaped[..., 0, :, 0, :] + shaped[..., 1, :, 1, :]
    imag_part = shaped[..., 0, :, 1, :] - shaped[..., 1, :, 0, :]
    return jnp.stack([real_part, imag_part], -3)


def combine_plain(summed):
    real_part = summed[..., 0, 0, :] - summed[..., 1, 1, :]
    imag_part = summed[..., 0, 1, :] + summed[..., 1, 0, :]
    return jnp.stack([real_part, imag_part], -2)


def reference(wave_in, column_basis, row_basis, tile_scale, tile_ranks):
    blocks = RMAX // 16
    forward_list = []
    adjoint_list = []
    for freq_index in range(NF):
        wavefield = wave_in[freq_index].reshape(NT, NB, 2, NVS).astype(jnp.float32)
        live_mask = ((16 * jnp.arange(blocks, dtype=jnp.int32))[None, None, :] < tile_ranks[freq_index][:, :, None]).astype(jnp.float32)
        weights = tile_scale[freq_index][:, :, None] * live_mask
        column_bases = column_basis[freq_index]
        row_bases = row_basis[freq_index]

        def forward_step(running, column):
            column_tile = column_bases[:, column].astype(jnp.float32)
            products = jnp.einsum("mbc,bpn->mcpn", column_tile, wavefield[column], precision=lax.Precision.HIGHEST)
            coded_rows = combine_conj(products) * weights[:, column][:, :, None, None, None]
            coded_rows = lax.optimization_barrier(coded_rows.astype(jnp.bfloat16)).astype(jnp.float32)
            row_tile = row_bases[:, column].astype(jnp.float32).reshape(MT, NB, blocks, 2, 16)
            summed = jnp.einsum("mbkqt,mkptn->mbqpn", row_tile, coded_rows, precision=lax.Precision.HIGHEST)
            return running + combine_plain(summed), None

        start_sum = jnp.zeros((MT, NB, 2, NVS), jnp.float32)
        forward_sum, _ = lax.scan(forward_step, start_sum, jnp.arange(NT, dtype=jnp.int32))
        forward = lax.optimization_barrier(forward_sum.astype(jnp.bfloat16))
        forward_wide = forward.astype(jnp.float32)

        def adjoint_step(running, row_index):
            row_tile = row_bases[row_index].astype(jnp.float32)
            products = jnp.einsum("jbc,bpn->jcpn", row_tile, forward_wide[row_index], precision=lax.Precision.HIGHEST)
            returned = combine_conj(products) * weights[row_index][:, :, None, None, None]
            returned = lax.optimization_barrier(returned.astype(jnp.bfloat16)).astype(jnp.float32)
            column_tile = column_bases[row_index].astype(jnp.float32).reshape(NT, NB, blocks, 2, 16)
            summed = jnp.einsum("jbkqt,jkptn->jbqpn", column_tile, returned, precision=lax.Precision.HIGHEST)
            return running + combine_plain(summed), None

        start_adj = jnp.zeros((NT, NB, 2, NVS), jnp.float32)
        adjoint_sum, _ = lax.scan(adjoint_step, start_adj, jnp.arange(MT, dtype=jnp.int32))
        forward_list.append(forward.reshape(MT * NB, 2, NVS))
        adjoint_list.append(adjoint_sum.astype(jnp.bfloat16).reshape(NT * NB, 2, NVS))
    return jnp.stack(forward_list), jnp.stack(adjoint_list)
```

```python
import functools
import jax
import jax.numpy as jnp
from jax import lax
from jax.experimental import pallas as pl
from jax.experimental.pallas import tpu as pltpu
from jax.sharding import PartitionSpec as P

NB = 256
RMAX = 64
NVS = 256
TILES = 64
BLOCKS = RMAX // 16
WIDTH = 2 * RMAX
SLOTS = 5
ROWS = 32 * SLOTS
GROUP = 4
CHUNKS = TILES // GROUP
STRIDE = 27
MESH = pl.DeviceIdType.MESH
BF16 = jnp.bfloat16
F32 = jnp.float32


def offset_of(step):
    mixed = lax.rem((step + 1) * STRIDE, TILES)
    return mixed // 16, lax.rem(mixed // 4, 4), lax.rem(mixed, 4)


def shifted(me, step, sign):
    dy, dx, dz = offset_of(step)
    y, x, z = me // 16, lax.rem(me // 4, 4), lax.rem(me, 4)
    y = lax.rem(y + sign * dy + 4, 4)
    x = lax.rem(x + sign * dx + 4, 4)
    z = lax.rem(z + sign * dz + 4, 4)
    return (y * 4 + x) * 4 + z


def conj_block(products, block):
    top = products[32 * block : 32 * block + 16]
    low = products[32 * block + 16 : 32 * block + 32]
    real = top[:, :NVS] + low[:, NVS:]
    imag = top[:, NVS:] - low[:, :NVS]
    return jnp.concatenate([real, imag], 0)


def pack(products0, products1, rank0, rank1, scale0, scale1):
    slots = []
    for slot in range(SLOTS):
        value = None
        if slot < BLOCKS:
            weight = jnp.where(16 * slot < rank0, scale0, 0.0)
            value = conj_block(products0, slot) * weight
        if slot > 0:
            block = SLOTS - 1 - slot
            weight = jnp.where(16 * block < rank1, scale1, 0.0)
            other = conj_block(products1, block) * weight
            value = other if value is None else value + other
        slots.append(value.astype(BF16))
    return jnp.concatenate(slots, 0)


def unpack(packed, rank0, rank1):
    first, second = [], []
    for slot in range(SLOTS):
        real = packed[32 * slot : 32 * slot + 16]
        imag = packed[32 * slot + 16 : 32 * slot + 32]
        both = jnp.concatenate(
            [jnp.concatenate([real, imag], 1), jnp.concatenate([-imag, real], 1)], 0
        )
        if slot < BLOCKS:
            live = jnp.where(16 * slot < rank0, 1.0, 0.0).astype(BF16)
            first.append(both if slot == 0 else both * live)
        if slot > 0:
            block = SLOTS - 1 - slot
            live = jnp.where(16 * block < rank1, 1.0, 0.0).astype(BF16)
            second.append(both if block == 0 else both * live)
    return jnp.concatenate(first, 0), jnp.concatenate(second[::-1], 0)


def body(
    wave_ref, col_hbm, row_hbm, scale_ref, rank_ref,
    fwd_ref, adj_ref,
    vbuf, ubuf, xs, xmat, ybuf, send1, recv1, send2, recv2, dense, acc, halves, landed,
    vsem, usem, ssem1, rsem1, ssem2, rsem2, xsems,
):
    me = lax.axis_index("tile")
    f = lax.axis_index("freq")
    partner = {"freq": 1 - f}

    def v_copy(step):
        d = shifted(me, step, 1)
        return pltpu.make_async_copy(col_hbm.at[d], vbuf.at[d], vsem.at[step])

    def u_copy(part):
        span = pl.ds(part * 16, 16)
        return pltpu.make_async_copy(
            row_hbm.at[:, span], ubuf.at[:, span], usem.at[part]
        )

    @pl.loop(0, TILES)
    def _(step):
        v_copy(step).start()

    barrier = pltpu.get_barrier_semaphore()
    pl.semaphore_signal(barrier, inc=1, device_id=partner, device_id_type=MESH)

    @pl.loop(0, TILES - 1)
    def _(step):
        pl.semaphore_signal(
            barrier, inc=1, device_id={"tile": shifted(me, step, 1)}, device_id_type=MESH
        )

    pl.semaphore_wait(barrier, TILES)

    x_copy = pltpu.make_async_remote_copy(
        src_ref=wave_ref.at[1 - f], dst_ref=xs, send_sem=xsems.at[0],
        recv_sem=xsems.at[1], device_id=partner, device_id_type=MESH,
    )
    x_copy.start()
    for part in range(4):
        u_copy(part).start()
    x_copy.wait()
    mine, theirs = wave_ref[f], xs[...]
    for p in range(2):
        low = jnp.where(f == 0, mine[p], theirs[p])
        high = jnp.where(f == 0, theirs[p], mine[p])
        xmat[:, p * NVS : p * NVS + 128] = low
        xmat[:, p * NVS + 128 : (p + 1) * NVS] = high

    def transfer(send, recv, ssem, rsem, step):
        return pltpu.make_async_remote_copy(
            src_ref=send.at[step], dst_ref=recv.at[step], send_sem=ssem.at[step],
            recv_sem=rsem.at[step], device_id={"tile": shifted(me, step, 1)},
            device_id_type=MESH,
        )

    def deliver(send, recv, ssem, rsem, chunk, values):
        for k in range(GROUP):
            if k < GROUP - 1:
                send[chunk * GROUP + k] = values[k]
        if GROUP > 0:
            last = chunk * GROUP + GROUP - 1

            @pl.when(chunk < CHUNKS - 1)
            def _():
                send[last] = values[GROUP - 1]

            @pl.when(chunk == CHUNKS - 1)
            def _():
                recv[last] = values[GROUP - 1]

        for k in range(GROUP):
            step = chunk * GROUP + k

            @pl.when(step < TILES - 1)
            def _():
                transfer(send, recv, ssem, rsem, step).start()

    def arrive(send, recv, ssem, rsem, chunk):
        for k in range(GROUP):
            step = chunk * GROUP + k

            @pl.when(step < TILES - 1)
            def _():
                transfer(send, recv, ssem, rsem, step).wait_recv()

    def contract(left, right):
        return lax.dot_general(
            left, right, (((0,), (0,)), ((), ())), preferred_element_type=F32
        )

    @pl.loop(0, CHUNKS)
    def _(chunk):
        ids = [shifted(me, chunk * GROUP + k, 1) for k in range(GROUP)]
        for k in range(GROUP):
            v_copy(chunk * GROUP + k).wait()
        left = jnp.concatenate([vbuf[d, r] for d in ids for r in range(2)], 1)
        products = contract(left, xmat[...])
        values = []
        for k, d in enumerate(ids):
            at = 2 * k * WIDTH
            values.append(
                pack(
                    products[at : at + WIDTH], products[at + WIDTH : at + 2 * WIDTH],
                    rank_ref[2 * d, me], rank_ref[2 * d + 1, me],
                    scale_ref[2 * d, me], scale_ref[2 * d + 1, me],
                )
            )
        deliver(send1, recv1, ssem1, rsem1, chunk, values)

    for part in range(4):
        u_copy(part).wait()

    acc[...] = jnp.zeros_like(acc)

    @pl.loop(0, CHUNKS)
    def _(chunk):
        arrive(send1, recv1, ssem1, rsem1, chunk)
        ids = [shifted(me, chunk * GROUP + k, -1) for k in range(GROUP)]
        for k, j in enumerate(ids):
            first, second = unpack(
                recv1[chunk * GROUP + k], rank_ref[2 * me, j], rank_ref[2 * me + 1, j]
            )
            dense[k * WIDTH : (k + 1) * WIDTH] = first
            dense[(GROUP + k) * WIDTH : (GROUP + k + 1) * WIDTH] = second
        for r in range(2):
            left = jnp.concatenate([ubuf[r, j] for j in ids], 1)
            right = dense[r * GROUP * WIDTH : (r + 1) * GROUP * WIDTH]
            acc[r] += jnp.dot(left, right, preferred_element_type=F32)

    for r in range(2):
        ybuf[r] = acc[r].astype(BF16)

    @pl.loop(0, CHUNKS)
    def _(chunk):
        ids = [shifted(me, chunk * GROUP + k, 1) for k in range(GROUP)]
        products = [
            contract(jnp.concatenate([ubuf[r, j] for j in ids], 1), ybuf[r])
            for r in range(2)
        ]
        values = []
        for k, j in enumerate(ids):
            at = k * WIDTH
            values.append(
                pack(
                    products[0][at : at + WIDTH], products[1][at : at + WIDTH],
                    rank_ref[2 * me, j], rank_ref[2 * me + 1, j],
                    scale_ref[2 * me, j], scale_ref[2 * me + 1, j],
                )
            )
        deliver(send2, recv2, ssem2, rsem2, chunk, values)

    for r in range(2):
        for p in range(2):
            fwd_ref[r, p] = ybuf[r, :, p * NVS : (p + 1) * NVS]
    acc[0] = jnp.zeros((NB, 2 * NVS), F32)

    @pl.loop(0, CHUNKS)
    def _(chunk):
        arrive(send2, recv2, ssem2, rsem2, chunk)
        ids = [shifted(me, chunk * GROUP + k, -1) for k in range(GROUP)]
        for k, d in enumerate(ids):
            first, second = unpack(
                recv2[chunk * GROUP + k], rank_ref[2 * d, me], rank_ref[2 * d + 1, me]
            )
            dense[2 * k * WIDTH : (2 * k + 1) * WIDTH] = first
            dense[(2 * k + 1) * WIDTH : (2 * k + 2) * WIDTH] = second
        left = jnp.concatenate([vbuf[d, r] for d in ids for r in range(2)], 1)
        acc[0] += jnp.dot(left, dense[...], preferred_element_type=F32)

    for half in range(2):
        for p in range(2):
            at = p * NVS + half * 128
            halves[half, p] = acc[0, :, at : at + 128].astype(BF16)
    out_copy = pltpu.make_async_remote_copy(
        src_ref=halves.at[1 - f], dst_ref=landed, send_sem=xsems.at[2],
        recv_sem=xsems.at[3], device_id=partner, device_id_type=MESH,
    )
    out_copy.start()
    adj_ref[f] = halves[f]

    @pl.loop(0, TILES - 1)
    def _(step):
        transfer(send1, recv1, ssem1, rsem1, step).wait_send()
        transfer(send2, recv2, ssem2, rsem2, step).wait_send()

    out_copy.wait()
    adj_ref[1 - f] = landed[...]


def per_device(wave_in, column_basis, row_basis, tile_scale, tile_ranks):
    wave = jnp.transpose(wave_in, (0, 2, 1, 3))
    columns = column_basis.reshape(TILES, 2, NB, WIDTH)
    rows = row_basis.reshape(2, TILES, NB, WIDTH)
    anywhere = pl.BlockSpec(memory_space=pl.ANY)
    vmem = pl.BlockSpec(memory_space=pltpu.VMEM)
    smem = pl.BlockSpec(memory_space=pltpu.SMEM)
    packed = pltpu.VMEM((TILES, ROWS, NVS), BF16)
    forward, adjoint = pl.pallas_call(
        body,
        out_shape=(
            jax.ShapeDtypeStruct((2, 2, NB, NVS), BF16),
            jax.ShapeDtypeStruct((2, 2, NB, 128), BF16),
        ),
        in_specs=[vmem, anywhere, anywhere, smem, smem],
        out_specs=(vmem, vmem),
        scratch_shapes=[
            pltpu.VMEM((TILES, 2, NB, WIDTH), BF16),
            pltpu.VMEM((2, TILES, NB, WIDTH), BF16),
            pltpu.VMEM((2, NB, 128), BF16),
            pltpu.VMEM((NB, 2 * NVS), BF16),
            pltpu.VMEM((2, NB, 2 * NVS), BF16),
            packed, packed, packed, packed,
            pltpu.VMEM((2 * GROUP * WIDTH, 2 * NVS), BF16),
            pltpu.VMEM((2, NB, 2 * NVS), F32),
            pltpu.VMEM((2, 2, NB, 128), BF16),
            pltpu.VMEM((2, NB, 128), BF16),
            pltpu.SemaphoreType.DMA((TILES,)),
            pltpu.SemaphoreType.DMA((4,)),
            pltpu.SemaphoreType.DMA((TILES,)),
            pltpu.SemaphoreType.DMA((TILES,)),
            pltpu.SemaphoreType.DMA((TILES,)),
            pltpu.SemaphoreType.DMA((TILES,)),
            pltpu.SemaphoreType.DMA((4,)),
        ],
        compiler_params=pltpu.CompilerParams(
            collective_id=0, has_side_effects=True, vmem_limit_bytes=63 << 20
        ),
        name="normal_operator",
    )(wave, columns, rows, tile_scale[0], tile_ranks[0])
    forward_out = jnp.transpose(forward, (0, 2, 1, 3)).reshape(1, 2 * NB, 2, NVS)
    adjoint_out = jnp.transpose(adjoint, (0, 2, 1, 3))
    return forward_out, adjoint_out


def solution(mesh):
    return jax.shard_map(
        per_device,
        mesh=mesh,
        in_specs=(
            P(None, "tile", None, "freq"),
            P("freq", None, "tile", None, None),
            P("freq", "tile", None, None, None),
            P("freq", None, None),
            P("freq", None, None),
        ),
        out_specs=(P("freq", "tile", None, None), P(None, "tile", None, "freq")),
        check_vma=False,
    )
```

```python
import functools
import jax
import jax.numpy as jnp
from jax import lax
from jax.experimental import pallas as pl
from jax.experimental.pallas import tpu as pltpu
from jax.sharding import PartitionSpec as P

NB = 256
RMAX = 64
NVS = 256
TILES = 64
HALF = NVS // 2
BLOCKS = RMAX // 16
WIDTH = 2 * RMAX
SLOTS = 5
ROWS = 32 * SLOTS
GROUP = 4
CHUNKS = TILES // GROUP
STRIDE = 27
MESH = pl.DeviceIdType.MESH
BF16 = jnp.bfloat16
F32 = jnp.float32


def offset_of(step):
    mixed = lax.rem((step + 1) * STRIDE, TILES)
    return mixed // 16, lax.rem(mixed // 4, 4), lax.rem(mixed, 4)


def shifted(me, step, sign):
    dy, dx, dz = offset_of(step)
    y, x, z = me // 16, lax.rem(me // 4, 4), lax.rem(me, 4)
    y = lax.rem(y + sign * dy + 4, 4)
    x = lax.rem(x + sign * dx + 4, 4)
    z = lax.rem(z + sign * dz + 4, 4)
    return (y * 4 + x) * 4 + z


def conj_block(products, block):
    top = products[32 * block : 32 * block + 16]
    low = products[32 * block + 16 : 32 * block + 32]
    real = top[:, :HALF] + low[:, HALF:]
    imag = top[:, HALF:] - low[:, :HALF]
    return jnp.concatenate([real, imag], 0)


def pack(products0, products1, rank0, rank1, scale0, scale1):
    slots = []
    for slot in range(SLOTS):
        value = None
        if slot < BLOCKS:
            weight = jnp.where(16 * slot < rank0, scale0, 0.0)
            value = conj_block(products0, slot) * weight
        if slot > 0:
            block = SLOTS - 1 - slot
            weight = jnp.where(16 * block < rank1, scale1, 0.0)
            other = conj_block(products1, block) * weight
            value = other if value is None else value + other
        slots.append(value.astype(BF16))
    return jnp.concatenate(slots, 0)


def unpack(packed, rank0, rank1):
    first, second = [], []
    for slot in range(SLOTS):
        real = packed[32 * slot : 32 * slot + 16]
        imag = packed[32 * slot + 16 : 32 * slot + 32]
        both = jnp.concatenate(
            [jnp.concatenate([real, imag], 1), jnp.concatenate([-imag, real], 1)], 0
        )
        if slot < BLOCKS:
            live = jnp.where(16 * slot < rank0, 1.0, 0.0).astype(BF16)
            first.append(both if slot == 0 else both * live)
        if slot > 0:
            block = SLOTS - 1 - slot
            live = jnp.where(16 * block < rank1, 1.0, 0.0).astype(BF16)
            second.append(both if block == 0 else both * live)
    return jnp.concatenate(first, 0), jnp.concatenate(second[::-1], 0)


def body(
    wave_ref, col_hbm, row_hbm, scale_ref, rank_ref,
    fwd_ref, adj_ref,
    vbuf, ubuf, landing, xmat, ybuf, send, recv, dense, acc, leaving, landed,
    vsem, usem, ssem, rsem, xsems,
):
    me = lax.axis_index("tile")
    f = lax.axis_index("freq")
    partner = {"freq": 1 - f}
    last = TILES - 1

    def v_copy(step, d):
        return pltpu.make_async_copy(col_hbm.at[d], vbuf.at[d], vsem.at[step])

    def u_copy(part):
        span = pl.ds(part * 16, 16)
        return pltpu.make_async_copy(
            row_hbm.at[:, span], ubuf.at[:, span], usem.at[part]
        )

    barrier = pltpu.get_barrier_semaphore()
    pl.semaphore_signal(barrier, inc=1, device_id=partner, device_id_type=MESH)
    ys = [16 * lax.rem(me // 16 + k, 4) for k in range(4)]
    xs = [4 * lax.rem(me // 4 + k, 4) for k in range(4)]
    zs = [lax.rem(me + k, 4) for k in range(4)]
    for step in range(TILES):
        mixed = (step + 1) * STRIDE % TILES
        d = ys[mixed // 16] + xs[mixed // 4 % 4] + zs[mixed % 4]
        if step < last:
            pl.semaphore_signal(
                barrier, inc=1, device_id={"tile": d}, device_id_type=MESH
            )
        v_copy(step, d).start()
    for part in range(4):
        u_copy(part).start()

    def targets(chunk, sign):
        return [shifted(me, chunk * GROUP + k, sign) for k in range(GROUP)]

    def transfer(phase, step):
        return pltpu.make_async_remote_copy(
            src_ref=send.at[phase, step], dst_ref=recv.at[phase, step],
            send_sem=ssem.at[phase, step], recv_sem=rsem.at[phase, step],
            device_id={"tile": shifted(me, step, 1)}, device_id_type=MESH,
        )

    def store(phase, chunk, values):
        for k in range(GROUP):
            send[phase, chunk * GROUP + k] = values[k]

        @pl.when(chunk == CHUNKS - 1)
        def _():
            recv[phase, last] = values[GROUP - 1]

    def depart(phase, chunk):
        for k in range(GROUP - 1):
            transfer(phase, chunk * GROUP + k).start()

        @pl.when(chunk < CHUNKS - 1)
        def _():
            transfer(phase, chunk * GROUP + GROUP - 1).start()

    def arrive(phase, chunk):
        for k in range(GROUP - 1):
            transfer(phase, chunk * GROUP + k).wait_recv()

        @pl.when(chunk < CHUNKS - 1)
        def _():
            transfer(phase, chunk * GROUP + GROUP - 1).wait_recv()

    def sent(phase):
        @pl.loop(0, last)
        def _(step):
            transfer(phase, step).wait_send()

    def contract(left, right):
        return lax.dot_general(
            left, right, (((0,), (0,)), ((), ())), preferred_element_type=F32
        )

    def code(half, chunk):
        ids = targets(chunk, 1)
        left = jnp.concatenate([vbuf[d, r] for d in ids for r in range(2)], 1)
        products = contract(left, xmat[half])
        values = []
        for k, d in enumerate(ids):
            at = 2 * k * WIDTH
            values.append(
                pack(
                    products[at : at + WIDTH], products[at + WIDTH : at + 2 * WIDTH],
                    rank_ref[me, 2 * d], rank_ref[me, 2 * d + 1],
                    scale_ref[me, 2 * d], scale_ref[me, 2 * d + 1],
                )
            )
        store(half, chunk, values)

    def loaded(chunk):
        for k in range(GROUP):
            v_copy(chunk * GROUP + k, 0).wait()

    def expand(half):
        acc[...] = jnp.zeros_like(acc)

        @pl.loop(0, CHUNKS)
        def _(chunk):
            arrive(half, chunk)
            ids = targets(chunk, -1)
            for k, j in enumerate(ids):
                first, second = unpack(
                    recv[half, chunk * GROUP + k],
                    rank_ref[j, 2 * me], rank_ref[j, 2 * me + 1],
                )
                dense[k * WIDTH : (k + 1) * WIDTH] = first
                dense[(GROUP + k) * WIDTH : (GROUP + k + 1) * WIDTH] = second
            for r in range(2):
                left = jnp.concatenate([ubuf[r, j] for j in ids], 1)
                right = dense[r * GROUP * WIDTH : (r + 1) * GROUP * WIDTH]
                acc[r] += jnp.dot(left, right, preferred_element_type=F32)

        for r in range(2):
            ybuf[half, r] = acc[r].astype(BF16)

    def code_back(half):
        @pl.loop(0, CHUNKS)
        def _(chunk):
            ids = targets(chunk, 1)
            products = [
                contract(
                    jnp.concatenate([ubuf[r, j] for j in ids], 1), ybuf[half, r]
                )
                for r in range(2)
            ]
            values = []
            for k, j in enumerate(ids):
                at = k * WIDTH
                values.append(
                    pack(
                        products[0][at : at + WIDTH], products[1][at : at + WIDTH],
                        rank_ref[j, 2 * me], rank_ref[j, 2 * me + 1],
                        scale_ref[j, 2 * me], scale_ref[j, 2 * me + 1],
                    )
                )
            store(2 + half, chunk, values)
            depart(2 + half, chunk)

    def expand_back(half):
        acc[0] = jnp.zeros((NB, NVS), F32)

        @pl.loop(0, CHUNKS)
        def _(chunk):
            arrive(2 + half, chunk)
            ids = targets(chunk, -1)
            for k, d in enumerate(ids):
                first, second = unpack(
                    recv[2 + half, chunk * GROUP + k],
                    rank_ref[me, 2 * d], rank_ref[me, 2 * d + 1],
                )
                dense[2 * k * WIDTH : (2 * k + 1) * WIDTH] = first
                dense[(2 * k + 1) * WIDTH : (2 * k + 2) * WIDTH] = second
            left = jnp.concatenate([vbuf[d, r] for d in ids for r in range(2)], 1)
            acc[0] += jnp.dot(left, dense[...], preferred_element_type=F32)

    for p in range(2):
        xmat[0, :, p * HALF : (p + 1) * HALF] = wave_ref[f, p]
    loaded(0)
    code(0, 0)
    pl.semaphore_wait(barrier, TILES)
    depart(0, 0)
    x_copy = pltpu.make_async_remote_copy(
        src_ref=wave_ref.at[1 - f], dst_ref=landing, send_sem=xsems.at[0],
        recv_sem=xsems.at[1], device_id=partner, device_id_type=MESH,
    )
    x_copy.start()

    @pl.loop(1, CHUNKS)
    def _(chunk):
        loaded(chunk)
        code(0, chunk)
        depart(0, chunk)

    x_copy.wait()
    for p in range(2):
        xmat[1, :, p * HALF : (p + 1) * HALF] = landing[p]

    @pl.loop(0, CHUNKS)
    def _(chunk):
        code(1, chunk)
        depart(1, chunk)

    for part in range(4):
        u_copy(part).wait()
    expand(0)
    code_back(0)
    expand(1)
    code_back(1)
    for r in range(2):
        for p in range(2):
            own = ybuf[0, r, :, p * HALF : (p + 1) * HALF]
            other = ybuf[1, r, :, p * HALF : (p + 1) * HALF]
            rows = slice(r * NB, (r + 1) * NB)
            fwd_ref[p, rows, :HALF] = jnp.where(f == 0, own, other)
            fwd_ref[p, rows, HALF:] = jnp.where(f == 0, other, own)
    sent(0)
    sent(1)
    expand_back(0)
    for p in range(2):
        adj_ref[f, p] = acc[0, :, p * HALF : (p + 1) * HALF].astype(BF16)
    expand_back(1)
    for p in range(2):
        leaving[p] = acc[0, :, p * HALF : (p + 1) * HALF].astype(BF16)
    out_copy = pltpu.make_async_remote_copy(
        src_ref=leaving, dst_ref=landed, send_sem=xsems.at[2],
        recv_sem=xsems.at[3], device_id=partner, device_id_type=MESH,
    )
    out_copy.start()
    sent(2)
    sent(3)
    out_copy.wait()
    adj_ref[1 - f] = landed[...]


def per_device(wave_in, column_basis, row_basis, tile_scale, tile_ranks):
    wave = jnp.transpose(wave_in, (0, 2, 1, 3))
    columns = column_basis.reshape(TILES, 2, NB, WIDTH)
    rows = row_basis.reshape(2, TILES, NB, WIDTH)
    anywhere = pl.BlockSpec(memory_space=pl.ANY)
    vmem = pl.BlockSpec(memory_space=pltpu.VMEM)
    smem = pl.BlockSpec(memory_space=pltpu.SMEM)
    packed = pltpu.VMEM((4, TILES, ROWS, HALF), BF16)
    forward, adjoint = pl.pallas_call(
        body,
        out_shape=(
            jax.ShapeDtypeStruct((2, 2 * NB, NVS), BF16),
            jax.ShapeDtypeStruct((2, 2, NB, HALF), BF16),
        ),
        in_specs=[vmem, anywhere, anywhere, smem, smem],
        out_specs=(vmem, vmem),
        scratch_shapes=[
            pltpu.VMEM((TILES, 2, NB, WIDTH), BF16),
            pltpu.VMEM((2, TILES, NB, WIDTH), BF16),
            pltpu.VMEM((2, NB, HALF), BF16),
            pltpu.VMEM((2, NB, NVS), BF16),
            pltpu.VMEM((2, 2, NB, NVS), BF16),
            packed, packed,
            pltpu.VMEM((2 * GROUP * WIDTH, NVS), BF16),
            pltpu.VMEM((2, NB, NVS), F32),
            pltpu.VMEM((2, NB, HALF), BF16),
            pltpu.VMEM((2, NB, HALF), BF16),
            pltpu.SemaphoreType.DMA((TILES,)),
            pltpu.SemaphoreType.DMA((4,)),
            pltpu.SemaphoreType.DMA((4, TILES)),
            pltpu.SemaphoreType.DMA((4, TILES)),
            pltpu.SemaphoreType.DMA((4,)),
        ],
        compiler_params=pltpu.CompilerParams(
            collective_id=0, has_side_effects=True, vmem_limit_bytes=63 << 20
        ),
        name="normal_operator",
    )(wave, columns, rows, tile_scale[0].T, tile_ranks[0].T)
    forward_out = jnp.transpose(forward, (1, 0, 2))[None]
    adjoint_out = jnp.transpose(adjoint, (0, 2, 1, 3))
    return forward_out, adjoint_out


def solution(mesh):
    return jax.shard_map(
        per_device,
        mesh=mesh,
        in_specs=(
            P(None, "tile", None, "freq"),
            P("freq", None, "tile", None, None),
            P("freq", "tile", None, None, None),
            P("freq", None, None),
            P("freq", None, None),
        ),
        out_specs=(P("freq", "tile", None, None), P(None, "tile", None, "freq")),
        check_vma=False,
    )
```

```python
import functools
import jax
import jax.numpy as jnp
from jax import lax
from jax.experimental import pallas as pl
from jax.experimental.pallas import tpu as pltpu
from jax.sharding import PartitionSpec as P

NB = 256
RMAX = 64
NVS = 256
TILES = 64
HALF = NVS // 2
BLOCKS = RMAX // 16
WIDTH = 2 * RMAX
SLOTS = 5
ROWS = 32 * SLOTS
GROUP = 4
CHUNKS = TILES // GROUP
STRIDE = 5
MESH = pl.DeviceIdType.MESH
BF16 = jnp.bfloat16
F32 = jnp.float32


def offset_of(step):
    mixed = lax.rem((step + 1) * STRIDE, TILES)
    return mixed // 16, lax.rem(mixed // 4, 4), lax.rem(mixed, 4)


def shifted(me, step, sign):
    dy, dx, dz = offset_of(step)
    y, x, z = me // 16, lax.rem(me // 4, 4), lax.rem(me, 4)
    y = lax.rem(y + sign * dy + 4, 4)
    x = lax.rem(x + sign * dx + 4, 4)
    z = lax.rem(z + sign * dz + 4, 4)
    return (y * 4 + x) * 4 + z


def conj_block(products, block):
    top = products[32 * block : 32 * block + 16]
    low = products[32 * block + 16 : 32 * block + 32]
    real = top[:, :HALF] + low[:, HALF:]
    imag = top[:, HALF:] - low[:, :HALF]
    return jnp.concatenate([real, imag], 0)


def pack(products0, products1, rank0, rank1, scale0, scale1):
    slots = []
    for slot in range(SLOTS):
        value = None
        if slot < BLOCKS:
            weight = jnp.where(16 * slot < rank0, scale0, 0.0)
            value = conj_block(products0, slot) * weight
        if slot > 0:
            block = SLOTS - 1 - slot
            weight = jnp.where(16 * block < rank1, scale1, 0.0)
            other = conj_block(products1, block) * weight
            value = other if value is None else value + other
        slots.append(value.astype(BF16))
    return jnp.concatenate(slots, 0)


def unpack(packed, rank0, rank1):
    first, second = [], []
    for slot in range(SLOTS):
        real = packed[32 * slot : 32 * slot + 16]
        imag = packed[32 * slot + 16 : 32 * slot + 32]
        both = jnp.concatenate(
            [jnp.concatenate([real, imag], 1), jnp.concatenate([-imag, real], 1)], 0
        )
        if slot < BLOCKS:
            live = jnp.where(16 * slot < rank0, 1.0, 0.0).astype(BF16)
            first.append(both if slot == 0 else both * live)
        if slot > 0:
            block = SLOTS - 1 - slot
            live = jnp.where(16 * block < rank1, 1.0, 0.0).astype(BF16)
            second.append(both if block == 0 else both * live)
    return jnp.concatenate(first, 0), jnp.concatenate(second[::-1], 0)


def body(
    wave_hbm, col_hbm, row_hbm, scale_hbm, rank_hbm,
    fwd_hbm, adj_hbm,
    scale_ref, rank_ref, vbuf, ubuf, waves, xmat, ybuf, send, recv, dense, acc,
    stripes, fwdbuf, staying, leaving,
    vsem, usem, ssem, rsem, xsems, lsems,
):
    me = lax.axis_index("tile")
    f = lax.axis_index("freq")
    partner = {"freq": 1 - f}
    last = TILES - 1

    def v_copy(step, d):
        return pltpu.make_async_copy(col_hbm.at[d], vbuf.at[d], vsem.at[step])

    def u_copy(part):
        span = pl.ds(part * 16, 16)
        return pltpu.make_async_copy(
            row_hbm.at[:, span], ubuf.at[:, span], usem.at[part]
        )

    def own_rows(index):
        return pl.ds(pl.multiple_of(index * 2 * NB, 2 * NB), 2 * NB)

    barrier = pltpu.get_barrier_semaphore()
    ys = [16 * lax.rem(me // 16 + k, 4) for k in range(4)]
    xs = [4 * lax.rem(me // 4 + k, 4) for k in range(4)]
    zs = [lax.rem(me + k, 4) for k in range(4)]
    order = [(step + 1) * STRIDE % TILES for step in range(TILES)]
    ids = [ys[at // 16] + xs[at // 4 % 4] + zs[at % 4] for at in order]
    hops = [min(at // 16, 1) + min(at // 4 % 4, 1) + min(at % 4, 1)
            + (at // 16 == 2) + (at // 4 % 4 == 2) + (at % 4 == 2) for at in order]
    for step in sorted(range(last), key=lambda step: -hops[step]):
        pl.semaphore_signal(
            barrier, inc=1, device_id={"tile": ids[step]}, device_id_type=MESH
        )
    pl.semaphore_signal(barrier, inc=1, device_id=partner, device_id_type=MESH)
    table_copies = [
        pltpu.make_async_copy(scale_hbm, scale_ref, lsems.at[0]),
        pltpu.make_async_copy(rank_hbm, rank_ref, lsems.at[1]),
        pltpu.make_async_copy(wave_hbm.at[own_rows(f)], waves.at[0], lsems.at[2]),
    ]
    for copy in table_copies:
        copy.start()
    for step in range(TILES):
        v_copy(step, ids[step]).start()
    for part in range(4):
        u_copy(part).start()

    def targets(chunk, sign):
        return [shifted(me, chunk * GROUP + k, sign) for k in range(GROUP)]

    def transfer(phase, step):
        return pltpu.make_async_remote_copy(
            src_ref=send.at[phase, step], dst_ref=recv.at[phase, step],
            send_sem=ssem.at[phase, step], recv_sem=rsem.at[phase, step],
            device_id={"tile": shifted(me, step, 1)}, device_id_type=MESH,
        )

    def store(phase, chunk, values):
        for k in range(GROUP):
            send[phase, chunk * GROUP + k] = values[k]

        @pl.when(chunk == CHUNKS - 1)
        def _():
            recv[phase, last] = values[GROUP - 1]

    def depart(phase, chunk):
        for k in range(GROUP - 1):
            transfer(phase, chunk * GROUP + k).start()

        @pl.when(chunk < CHUNKS - 1)
        def _():
            transfer(phase, chunk * GROUP + GROUP - 1).start()

    def arrive(phase, chunk):
        for k in range(GROUP - 1):
            transfer(phase, chunk * GROUP + k).wait_recv()

        @pl.when(chunk < CHUNKS - 1)
        def _():
            transfer(phase, chunk * GROUP + GROUP - 1).wait_recv()

    def sent(phase):
        @pl.loop(0, last)
        def _(step):
            transfer(phase, step).wait_send()

    def contract(left, right):
        return lax.dot_general(
            left, right, (((0,), (0,)), ((), ())), preferred_element_type=F32
        )

    def code(half, chunk):
        ids = targets(chunk, 1)
        left = jnp.concatenate([vbuf[d, r] for d in ids for r in range(2)], 1)
        products = contract(left, xmat[half])
        values = []
        for k, d in enumerate(ids):
            at = 2 * k * WIDTH
            values.append(
                pack(
                    products[at : at + WIDTH], products[at + WIDTH : at + 2 * WIDTH],
                    rank_ref[me, 2 * d], rank_ref[me, 2 * d + 1],
                    scale_ref[me, 2 * d], scale_ref[me, 2 * d + 1],
                )
            )
        store(half, chunk, values)

    def loaded(chunk):
        for k in range(GROUP):
            v_copy(chunk * GROUP + k, 0).wait()

    def expand(half):
        acc[...] = jnp.zeros_like(acc)

        @pl.loop(0, CHUNKS)
        def _(chunk):
            arrive(half, chunk)
            ids = targets(chunk, -1)
            for k, j in enumerate(ids):
                first, second = unpack(
                    recv[half, chunk * GROUP + k],
                    rank_ref[j, 2 * me], rank_ref[j, 2 * me + 1],
                )
                dense[k * WIDTH : (k + 1) * WIDTH] = first
                dense[(GROUP + k) * WIDTH : (GROUP + k + 1) * WIDTH] = second
            for r in range(2):
                left = jnp.concatenate([ubuf[r, j] for j in ids], 1)
                right = dense[r * GROUP * WIDTH : (r + 1) * GROUP * WIDTH]
                acc[r] += jnp.dot(left, right, preferred_element_type=F32)

        for r in range(2):
            ybuf[half, r] = acc[r].astype(BF16)

    def code_back(half):
        @pl.loop(0, CHUNKS)
        def _(chunk):
            ids = targets(chunk, 1)
            products = [
                contract(
                    jnp.concatenate([ubuf[r, j] for j in ids], 1), ybuf[half, r]
                )
                for r in range(2)
            ]
            values = []
            for k, j in enumerate(ids):
                at = k * WIDTH
                values.append(
                    pack(
                        products[0][at : at + WIDTH], products[1][at : at + WIDTH],
                        rank_ref[j, 2 * me], rank_ref[j, 2 * me + 1],
                        scale_ref[j, 2 * me], scale_ref[j, 2 * me + 1],
                    )
                )
            store(2 + half, chunk, values)
            depart(2 + half, chunk)

    def expand_back(half):
        acc[0] = jnp.zeros((NB, NVS), F32)

        @pl.loop(0, CHUNKS)
        def _(chunk):
            arrive(2 + half, chunk)
            ids = targets(chunk, -1)
            for k, d in enumerate(ids):
                first, second = unpack(
                    recv[2 + half, chunk * GROUP + k],
                    rank_ref[me, 2 * d], rank_ref[me, 2 * d + 1],
                )
                dense[2 * k * WIDTH : (2 * k + 1) * WIDTH] = first
                dense[(2 * k + 1) * WIDTH : (2 * k + 2) * WIDTH] = second
            left = jnp.concatenate([vbuf[d, r] for d in ids for r in range(2)], 1)
            acc[0] += jnp.dot(left, dense[...], preferred_element_type=F32)

    def split(half):
        stripes[: 2 * NB] = waves[half].astype(F32)
        for p in range(2):
            part = stripes[pl.ds(p, NB, stride=2), :]
            xmat[half, :, p * HALF : (p + 1) * HALF] = part.astype(BF16)

    def merge(target):
        for p in range(2):
            stripes[pl.ds(p, NB, stride=2), :] = acc[0, :, p * HALF : (p + 1) * HALF]
        target[...] = stripes[: 2 * NB].astype(BF16)

    for copy in table_copies:
        copy.wait()
    split(0)
    loaded(0)
    code(0, 0)
    pl.semaphore_wait(barrier, TILES)
    depart(0, 0)
    x_copy = pltpu.make_async_remote_copy(
        src_ref=wave_hbm.at[own_rows(1 - f)], dst_ref=waves.at[1], send_sem=xsems.at[0],
        recv_sem=xsems.at[1], device_id=partner, device_id_type=MESH,
    )
    x_copy.start()

    @pl.loop(1, CHUNKS)
    def _(chunk):
        loaded(chunk)
        code(0, chunk)
        depart(0, chunk)

    x_copy.wait()
    split(1)

    @pl.loop(0, CHUNKS)
    def _(chunk):
        code(1, chunk)
        depart(1, chunk)

    for part in range(4):
        u_copy(part).wait()
    expand(0)
    code_back(0)
    expand(1)
    code_back(1)
    for r in range(2):
        for p in range(2):
            own = ybuf[0, r, :, p * HALF : (p + 1) * HALF].astype(F32)
            other = ybuf[1, r, :, p * HALF : (p + 1) * HALF].astype(F32)
            at = 4 * NB * r + p
            stripes[pl.ds(at, NB, stride=4), :] = jnp.where(f == 0, own, other)
            stripes[pl.ds(at + 2, NB, stride=4), :] = jnp.where(f == 0, other, own)
    fwdbuf[...] = stripes[...].astype(BF16)
    fwd_copy = pltpu.make_async_copy(fwdbuf, fwd_hbm, lsems.at[3])
    fwd_copy.start()
    sent(0)
    sent(1)
    expand_back(0)
    merge(staying)
    adj_copy = pltpu.make_async_copy(staying, adj_hbm.at[own_rows(f)], lsems.at[4])
    adj_copy.start()
    expand_back(1)
    merge(leaving)
    out_copy = pltpu.make_async_remote_copy(
        src_ref=leaving, dst_ref=adj_hbm.at[own_rows(f)], send_sem=xsems.at[2],
        recv_sem=xsems.at[3], device_id=partner, device_id_type=MESH,
    )
    out_copy.start()
    sent(2)
    sent(3)
    fwd_copy.wait()
    adj_copy.wait()
    out_copy.wait()


def per_device(wave_in, column_basis, row_basis, tile_scale, tile_ranks):
    wave = wave_in.reshape(4 * NB, HALF)
    columns = column_basis.reshape(TILES, 2, NB, WIDTH)
    rows = row_basis.reshape(2, TILES, NB, WIDTH)
    anywhere = pl.BlockSpec(memory_space=pl.ANY)
    packed = pltpu.VMEM((4, TILES, ROWS, HALF), BF16)
    forward, adjoint = pl.pallas_call(
        body,
        out_shape=(
            jax.ShapeDtypeStruct((8 * NB, HALF), BF16),
            jax.ShapeDtypeStruct((4 * NB, HALF), BF16),
        ),
        in_specs=[anywhere] * 5,
        out_specs=(anywhere, anywhere),
        scratch_shapes=[
            pltpu.SMEM((TILES, 2 * TILES), F32),
            pltpu.SMEM((TILES, 2 * TILES), jnp.int32),
            pltpu.VMEM((TILES, 2, NB, WIDTH), BF16),
            pltpu.VMEM((2, TILES, NB, WIDTH), BF16),
            pltpu.VMEM((2, 2 * NB, HALF), BF16),
            pltpu.VMEM((2, NB, NVS), BF16),
            pltpu.VMEM((2, 2, NB, NVS), BF16),
            packed, packed,
            pltpu.VMEM((2 * GROUP * WIDTH, NVS), BF16),
            pltpu.VMEM((2, NB, NVS), F32),
            pltpu.VMEM((8 * NB, HALF), F32),
            pltpu.VMEM((8 * NB, HALF), BF16),
            pltpu.VMEM((2 * NB, HALF), BF16),
            pltpu.VMEM((2 * NB, HALF), BF16),
            pltpu.SemaphoreType.DMA((TILES,)),
            pltpu.SemaphoreType.DMA((4,)),
            pltpu.SemaphoreType.DMA((4, TILES)),
            pltpu.SemaphoreType.DMA((4, TILES)),
            pltpu.SemaphoreType.DMA((4,)),
            pltpu.SemaphoreType.DMA((5,)),
        ],
        compiler_params=pltpu.CompilerParams(
            collective_id=0, has_side_effects=True, vmem_limit_bytes=56 << 20
        ),
        name="normal_operator",
    )(wave, columns, rows, tile_scale[0].T, tile_ranks[0].T)
    forward = forward.reshape(2 * NB, 2, 2, HALF).transpose(0, 2, 1, 3)
    forward_out = forward.reshape(1, 2 * NB, 2, NVS)
    adjoint_out = adjoint.reshape(2, NB, 2, HALF)
    return forward_out, adjoint_out


def solution(mesh):
    return jax.shard_map(
        per_device,
        mesh=mesh,
        in_specs=(
            P(None, "tile", None, "freq"),
            P("freq", None, "tile", None, None),
            P("freq", "tile", None, None, None),
            P("freq", None, None),
            P("freq", None, None),
        ),
        out_specs=(P("freq", "tile", None, None), P(None, "tile", None, "freq")),
        check_vma=False,
    )
```

```python
import functools
import jax
import jax.numpy as jnp
from jax import lax
from jax.experimental import pallas as pl
from jax.experimental.pallas import tpu as pltpu
from jax.sharding import PartitionSpec as P

NB = 256
RMAX = 64
NVS = 256
TILES = 64
HALF = NVS // 2
BLOCKS = RMAX // 16
WIDTH = 2 * RMAX
SLOTS = 5
ROWS = 32 * SLOTS
GROUP = 4
CHUNKS = TILES // GROUP
STRIDE = 5
OPPOSITE = next(s for s in range(TILES) if (s + 1) * STRIDE % TILES == 42)
MESH = pl.DeviceIdType.MESH
BF16 = jnp.bfloat16
F32 = jnp.float32


def nonzero(value):
    return (value * value + 4095) // 4096


def shifted(me, f, step, sign):
    mixed = lax.rem((step + 1) * STRIDE, TILES)
    dy, dx, dz = mixed // 16, lax.rem(mixed // 4, 4), lax.rem(mixed, 4)
    more = 2 * f * nonzero(step - OPPOSITE) * nonzero(step - (TILES - 1)) + 4
    y, x, z = me // 16, lax.rem(me // 4, 4), lax.rem(me, 4)
    y = lax.rem(y + sign * dy + more, 4)
    x = lax.rem(x + sign * dx + more, 4)
    z = lax.rem(z + sign * dz + more, 4)
    return (y * 4 + x) * 4 + z


def conj_block(products, block):
    top = products[32 * block : 32 * block + 16]
    low = products[32 * block + 16 : 32 * block + 32]
    real = top[:, :HALF] + low[:, HALF:]
    imag = top[:, HALF:] - low[:, :HALF]
    return jnp.concatenate([real, imag], 0)


def pack(products0, products1, rank0, rank1, scale0, scale1):
    slots = []
    for slot in range(SLOTS):
        value = None
        if slot < BLOCKS:
            weight = jnp.where(16 * slot < rank0, scale0, 0.0)
            value = conj_block(products0, slot) * weight
        if slot > 0:
            block = SLOTS - 1 - slot
            weight = jnp.where(16 * block < rank1, scale1, 0.0)
            other = conj_block(products1, block) * weight
            value = other if value is None else value + other
        slots.append(value.astype(BF16))
    return jnp.concatenate(slots, 0)


def unpack(packed, rank0, rank1):
    first, second = [], []
    for slot in range(SLOTS):
        real = packed[32 * slot : 32 * slot + 16]
        imag = packed[32 * slot + 16 : 32 * slot + 32]
        both = jnp.concatenate(
            [jnp.concatenate([real, imag], 1), jnp.concatenate([-imag, real], 1)], 0
        )
        if slot < BLOCKS:
            live = jnp.where(16 * slot < rank0, 1.0, 0.0).astype(BF16)
            first.append(both if slot == 0 else both * live)
        if slot > 0:
            block = SLOTS - 1 - slot
            live = jnp.where(16 * block < rank1, 1.0, 0.0).astype(BF16)
            second.append(both if block == 0 else both * live)
    return jnp.concatenate(first, 0), jnp.concatenate(second[::-1], 0)


def body(
    wave_hbm, col_hbm, row_hbm, scale_hbm, rank_hbm,
    fwd_ref, adj_ref,
    scale_ref, rank_ref, vbuf, ubuf, waves, xmat, ybuf, send, recv, dense, acc,
    stripes, leaving,
    vsem, usem, ssem, rsem, xsems, lsems,
):
    me = lax.axis_index("tile")
    f = lax.axis_index("freq")
    partner = {"freq": 1 - f}
    last = TILES - 1

    def v_copy(step, d):
        return pltpu.make_async_copy(col_hbm.at[d], vbuf.at[d], vsem.at[step])

    def u_copy(part):
        span = pl.ds(part * 16, 16)
        return pltpu.make_async_copy(
            row_hbm.at[:, span], ubuf.at[:, span], usem.at[part]
        )

    def own_rows(index):
        return pl.ds(pl.multiple_of(index * 2 * NB, 2 * NB), 2 * NB)

    barrier = pltpu.get_barrier_semaphore()
    turned = [
        (16 * lax.rem(me // 16 + more + k, 4), 4 * lax.rem(me // 4 + more + k, 4),
         lax.rem(me + more + k, 4))
        for more in (0, 2 * f) for k in range(4)
    ]
    order = [(step + 1) * STRIDE % TILES for step in range(TILES)]
    ids = []
    for step, at in enumerate(order):
        base = 0 if step in (OPPOSITE, last) else 4
        ids.append(
            turned[base + at // 16][0] + turned[base + at // 4 % 4][1]
            + turned[base + at % 4][2]
        )
    hops = [min(at // 16, 1) + min(at // 4 % 4, 1) + min(at % 4, 1)
            + (at // 16 == 2) + (at // 4 % 4 == 2) + (at % 4 == 2) for at in order]
    for step in sorted(range(last), key=lambda step: -hops[step]):
        pl.semaphore_signal(
            barrier, inc=1, device_id={"tile": ids[step]}, device_id_type=MESH
        )
    pl.semaphore_signal(barrier, inc=1, device_id=partner, device_id_type=MESH)
    table_copies = [
        pltpu.make_async_copy(scale_hbm, scale_ref, lsems.at[0]),
        pltpu.make_async_copy(rank_hbm, rank_ref, lsems.at[1]),
        pltpu.make_async_copy(wave_hbm.at[own_rows(f)], waves.at[0], lsems.at[2]),
    ]
    for copy in table_copies:
        copy.start()
    for step in range(TILES):
        v_copy(step, ids[step]).start()
    for part in range(4):
        u_copy(part).start()

    def targets(chunk, sign):
        return [shifted(me, f, chunk * GROUP + k, sign) for k in range(GROUP)]

    def transfer(phase, step):
        return pltpu.make_async_remote_copy(
            src_ref=send.at[phase, step], dst_ref=recv.at[phase, step],
            send_sem=ssem.at[phase, step], recv_sem=rsem.at[phase, step],
            device_id={"tile": shifted(me, f, step, 1)}, device_id_type=MESH,
        )

    def store(phase, chunk, values):
        for k in range(GROUP):
            send[phase, chunk * GROUP + k] = values[k]

        @pl.when(chunk == CHUNKS - 1)
        def _():
            recv[phase, last] = values[GROUP - 1]

    def depart(phase, chunk):
        for k in range(GROUP - 1):
            transfer(phase, chunk * GROUP + k).start()

        @pl.when(chunk < CHUNKS - 1)
        def _():
            transfer(phase, chunk * GROUP + GROUP - 1).start()

    def arrive(phase, chunk):
        for k in range(GROUP - 1):
            transfer(phase, chunk * GROUP + k).wait_recv()

        @pl.when(chunk < CHUNKS - 1)
        def _():
            transfer(phase, chunk * GROUP + GROUP - 1).wait_recv()

    def sent(phase):
        @pl.loop(0, last)
        def _(step):
            transfer(phase, step).wait_send()

    def contract(left, right):
        return lax.dot_general(
            left, right, (((0,), (0,)), ((), ())), preferred_element_type=F32
        )

    def code(half, chunk):
        ids = targets(chunk, 1)
        left = jnp.concatenate([vbuf[d, r] for d in ids for r in range(2)], 1)
        products = contract(left, xmat[half])
        values = []
        for k, d in enumerate(ids):
            at = 2 * k * WIDTH
            values.append(
                pack(
                    products[at : at + WIDTH], products[at + WIDTH : at + 2 * WIDTH],
                    rank_ref[me, 2 * d], rank_ref[me, 2 * d + 1],
                    scale_ref[me, 2 * d], scale_ref[me, 2 * d + 1],
                )
            )
        store(half, chunk, values)

    def loaded(chunk):
        for k in range(GROUP):
            v_copy(chunk * GROUP + k, 0).wait()

    def expand(half):
        acc[...] = jnp.zeros_like(acc)

        @pl.loop(0, CHUNKS)
        def _(chunk):
            arrive(half, chunk)
            ids = targets(chunk, -1)
            for k, j in enumerate(ids):
                first, second = unpack(
                    recv[half, chunk * GROUP + k],
                    rank_ref[j, 2 * me], rank_ref[j, 2 * me + 1],
                )
                dense[k * WIDTH : (k + 1) * WIDTH] = first
                dense[(GROUP + k) * WIDTH : (GROUP + k + 1) * WIDTH] = second
            for r in range(2):
                left = jnp.concatenate([ubuf[r, j] for j in ids], 1)
                right = dense[r * GROUP * WIDTH : (r + 1) * GROUP * WIDTH]
                acc[r] += jnp.dot(left, right, preferred_element_type=F32)

        for r in range(2):
            ybuf[half, r] = acc[r].astype(BF16)

    def code_back(half):
        @pl.loop(0, CHUNKS)
        def _(chunk):
            ids = targets(chunk, 1)
            products = [
                contract(
                    jnp.concatenate([ubuf[r, j] for j in ids], 1), ybuf[half, r]
                )
                for r in range(2)
            ]
            values = []
            for k, j in enumerate(ids):
                at = k * WIDTH
                values.append(
                    pack(
                        products[0][at : at + WIDTH], products[1][at : at + WIDTH],
                        rank_ref[j, 2 * me], rank_ref[j, 2 * me + 1],
                        scale_ref[j, 2 * me], scale_ref[j, 2 * me + 1],
                    )
                )
            store(2 + half, chunk, values)
            depart(2 + half, chunk)

    def expand_back(half):
        acc[0] = jnp.zeros((NB, NVS), F32)

        @pl.loop(0, CHUNKS)
        def _(chunk):
            arrive(2 + half, chunk)
            ids = targets(chunk, -1)
            for k, d in enumerate(ids):
                first, second = unpack(
                    recv[2 + half, chunk * GROUP + k],
                    rank_ref[me, 2 * d], rank_ref[me, 2 * d + 1],
                )
                dense[2 * k * WIDTH : (2 * k + 1) * WIDTH] = first
                dense[(2 * k + 1) * WIDTH : (2 * k + 2) * WIDTH] = second
            left = jnp.concatenate([vbuf[d, r] for d in ids for r in range(2)], 1)
            acc[0] += jnp.dot(left, dense[...], preferred_element_type=F32)

    def split(half):
        stripes[: 2 * NB] = waves[half].astype(F32)
        for p in range(2):
            part = stripes[pl.ds(p, NB, stride=2), :]
            xmat[half, :, p * HALF : (p + 1) * HALF] = part.astype(BF16)

    def merge(target):
        for p in range(2):
            stripes[pl.ds(p, NB, stride=2), :] = acc[0, :, p * HALF : (p + 1) * HALF]
        target[...] = stripes[: 2 * NB].astype(BF16)

    for copy in table_copies:
        copy.wait()
    split(0)
    loaded(0)
    code(0, 0)
    pl.semaphore_wait(barrier, TILES)
    depart(0, 0)
    x_copy = pltpu.make_async_remote_copy(
        src_ref=wave_hbm.at[own_rows(1 - f)], dst_ref=waves.at[1], send_sem=xsems.at[0],
        recv_sem=xsems.at[1], device_id=partner, device_id_type=MESH,
    )
    x_copy.start()

    @pl.loop(1, CHUNKS)
    def _(chunk):
        loaded(chunk)
        code(0, chunk)
        depart(0, chunk)

    x_copy.wait()
    split(1)

    @pl.loop(0, CHUNKS)
    def _(chunk):
        code(1, chunk)
        depart(1, chunk)

    for part in range(4):
        u_copy(part).wait()
    expand(0)
    code_back(0)
    expand(1)
    code_back(1)
    for r in range(2):
        for p in range(2):
            own = ybuf[0, r, :, p * HALF : (p + 1) * HALF].astype(F32)
            other = ybuf[1, r, :, p * HALF : (p + 1) * HALF].astype(F32)
            at = 4 * NB * r + p
            stripes[pl.ds(at, NB, stride=4), :] = jnp.where(f == 0, own, other)
            stripes[pl.ds(at + 2, NB, stride=4), :] = jnp.where(f == 0, other, own)
    fwd_ref[...] = stripes[...].astype(BF16)
    sent(0)
    sent(1)
    expand_back(0)
    merge(adj_ref.at[own_rows(f)])
    expand_back(1)
    merge(leaving)
    out_copy = pltpu.make_async_remote_copy(
        src_ref=leaving, dst_ref=adj_ref.at[own_rows(f)], send_sem=xsems.at[2],
        recv_sem=xsems.at[3], device_id=partner, device_id_type=MESH,
    )
    out_copy.start()
    sent(2)
    sent(3)
    out_copy.wait()


def hand_over(fwd_ref, adj_ref, fwd_hbm, adj_hbm, sems):
    copies = [
        pltpu.make_async_copy(fwd_ref, fwd_hbm, sems.at[0]),
        pltpu.make_async_copy(adj_ref, adj_hbm, sems.at[1]),
    ]
    for copy in copies:
        copy.start()
    for copy in copies:
        copy.wait()


def per_device(wave_in, column_basis, row_basis, tile_scale, tile_ranks):
    wave = wave_in.reshape(4 * NB, HALF)
    columns = column_basis.reshape(TILES, 2, NB, WIDTH)
    rows = row_basis.reshape(2, TILES, NB, WIDTH)
    anywhere = pl.BlockSpec(memory_space=pl.ANY)
    vmem = pl.BlockSpec(memory_space=pltpu.VMEM)
    packed = pltpu.VMEM((4, TILES, ROWS, HALF), BF16)
    forward, adjoint = pl.pallas_call(
        body,
        out_shape=(
            pltpu.VMEM((8 * NB, HALF), BF16),
            pltpu.VMEM((4 * NB, HALF), BF16),
        ),
        in_specs=[anywhere] * 5,
        out_specs=(vmem, vmem),
        scratch_shapes=[
            pltpu.SMEM((TILES, 2 * TILES), F32),
            pltpu.SMEM((TILES, 2 * TILES), jnp.int32),
            pltpu.VMEM((TILES, 2, NB, WIDTH), BF16),
            pltpu.VMEM((2, TILES, NB, WIDTH), BF16),
            pltpu.VMEM((2, 2 * NB, HALF), BF16),
            pltpu.VMEM((2, NB, NVS), BF16),
            pltpu.VMEM((2, 2, NB, NVS), BF16),
            packed, packed,
            pltpu.VMEM((2 * GROUP * WIDTH, NVS), BF16),
            pltpu.VMEM((2, NB, NVS), F32),
            pltpu.VMEM((8 * NB, HALF), F32),
            pltpu.VMEM((2 * NB, HALF), BF16),
            pltpu.SemaphoreType.DMA((TILES,)),
            pltpu.SemaphoreType.DMA((4,)),
            pltpu.SemaphoreType.DMA((4, TILES)),
            pltpu.SemaphoreType.DMA((4, TILES)),
            pltpu.SemaphoreType.DMA((4,)),
            pltpu.SemaphoreType.DMA((3,)),
        ],
        compiler_params=pltpu.CompilerParams(
            collective_id=0, has_side_effects=True, vmem_limit_bytes=56 << 20
        ),
        name="normal_operator",
    )(wave, columns, rows, tile_scale[0].T, tile_ranks[0].T)
    forward, adjoint = pl.pallas_call(
        hand_over,
        out_shape=(
            jax.ShapeDtypeStruct((8 * NB, HALF), BF16),
            jax.ShapeDtypeStruct((4 * NB, HALF), BF16),
        ),
        in_specs=[vmem, vmem],
        out_specs=(anywhere, anywhere),
        scratch_shapes=[pltpu.SemaphoreType.DMA((2,))],
        compiler_params=pltpu.CompilerParams(vmem_limit_bytes=4 << 20),
        name="hand_over",
    )(forward, adjoint)
    forward = forward.reshape(2 * NB, 2, 2, HALF).transpose(0, 2, 1, 3)
    forward_out = forward.reshape(1, 2 * NB, 2, NVS)
    adjoint_out = adjoint.reshape(2, NB, 2, HALF)
    return forward_out, adjoint_out


def solution(mesh):
    return jax.shard_map(
        per_device,
        mesh=mesh,
        in_specs=(
            P(None, "tile", None, "freq"),
            P("freq", None, "tile", None, None),
            P("freq", "tile", None, None, None),
            P("freq", None, None),
            P("freq", None, None),
        ),
        out_specs=(P("freq", "tile", None, None), P(None, "tile", None, "freq")),
        check_vma=False,
    )
```

```python
import functools
import jax
import jax.numpy as jnp
from jax import lax
from jax.experimental import pallas as pl
from jax.experimental.pallas import tpu as pltpu
from jax.sharding import PartitionSpec as P

NB = 256
RMAX = 64
NVS = 256
TILES = 64
HALF = NVS // 2
BLOCKS = RMAX // 16
WIDTH = 2 * RMAX
SLOTS = 5
ROWS = 32 * SLOTS
GROUP = 4
CHUNKS = TILES // GROUP
STRIDE = 27
MESH = pl.DeviceIdType.MESH
BF16 = jnp.bfloat16
F32 = jnp.float32


def offset_of(step):
    mixed = lax.rem((step + 1) * STRIDE, TILES)
    return mixed // 16, lax.rem(mixed // 4, 4), lax.rem(mixed, 4)


def shifted(me, step, sign):
    dy, dx, dz = offset_of(step)
    y, x, z = me // 16, lax.rem(me // 4, 4), lax.rem(me, 4)
    y = lax.rem(y + sign * dy + 4, 4)
    x = lax.rem(x + sign * dx + 4, 4)
    z = lax.rem(z + sign * dz + 4, 4)
    return (y * 4 + x) * 4 + z


def conj_block(products, block):
    top = products[32 * block : 32 * block + 16]
    low = products[32 * block + 16 : 32 * block + 32]
    real = top[:, :HALF] + low[:, HALF:]
    imag = top[:, HALF:] - low[:, :HALF]
    return jnp.concatenate([real, imag], 0)


def pack(products0, products1, rank0, rank1, scale0, scale1):
    slots = []
    for slot in range(SLOTS):
        value = None
        if slot < BLOCKS:
            weight = jnp.where(16 * slot < rank0, scale0, 0.0)
            value = conj_block(products0, slot) * weight
        if slot > 0:
            block = SLOTS - 1 - slot
            weight = jnp.where(16 * block < rank1, scale1, 0.0)
            other = conj_block(products1, block) * weight
            value = other if value is None else value + other
        slots.append(value.astype(BF16))
    return jnp.concatenate(slots, 0)


def unpack(packed, rank0, rank1):
    first, second = [], []
    for slot in range(SLOTS):
        real = packed[32 * slot : 32 * slot + 16]
        imag = packed[32 * slot + 16 : 32 * slot + 32]
        both = jnp.concatenate(
            [jnp.concatenate([real, imag], 1), jnp.concatenate([-imag, real], 1)], 0
        )
        if slot < BLOCKS:
            live = jnp.where(16 * slot < rank0, 1.0, 0.0).astype(BF16)
            first.append(both if slot == 0 else both * live)
        if slot > 0:
            block = SLOTS - 1 - slot
            live = jnp.where(16 * block < rank1, 1.0, 0.0).astype(BF16)
            second.append(both if block == 0 else both * live)
    return jnp.concatenate(first, 0), jnp.concatenate(second[::-1], 0)


def body(
    wave_hbm, col_hbm, row_hbm, scale_hbm, rank_hbm,
    fwd_ref, adj_ref,
    scale_ref, rank_ref, vbuf, ubuf, waves, xmat, ybuf, send, recv, dense, acc,
    stripes, leaving,
    vsem, usem, ssem, rsem, xsems, lsems,
):
    me = lax.axis_index("tile")
    f = lax.axis_index("freq")
    partner = {"freq": 1 - f}
    last = TILES - 1

    def v_copy(step, d):
        return pltpu.make_async_copy(col_hbm.at[d], vbuf.at[d], vsem.at[step])

    def u_copy(part):
        span = pl.ds(part * 16, 16)
        return pltpu.make_async_copy(
            row_hbm.at[:, span], ubuf.at[:, span], usem.at[part]
        )

    def own_rows(index):
        return pl.ds(pl.multiple_of(index * 2 * NB, 2 * NB), 2 * NB)

    barrier = pltpu.get_barrier_semaphore()
    ys = [16 * lax.rem(me // 16 + k, 4) for k in range(4)]
    xs = [4 * lax.rem(me // 4 + k, 4) for k in range(4)]
    zs = [lax.rem(me + k, 4) for k in range(4)]
    order = [(step + 1) * STRIDE % TILES for step in range(TILES)]
    ids = [ys[at // 16] + xs[at // 4 % 4] + zs[at % 4] for at in order]
    hops = [min(at // 16, 1) + min(at // 4 % 4, 1) + min(at % 4, 1)
            + (at // 16 == 2) + (at // 4 % 4 == 2) + (at % 4 == 2) for at in order]
    for step in sorted(range(last), key=lambda step: -hops[step]):
        pl.semaphore_signal(
            barrier, inc=1, device_id={"tile": ids[step]}, device_id_type=MESH
        )
    pl.semaphore_signal(barrier, inc=1, device_id=partner, device_id_type=MESH)
    table_copies = [
        pltpu.make_async_copy(scale_hbm, scale_ref, lsems.at[0]),
        pltpu.make_async_copy(rank_hbm, rank_ref, lsems.at[1]),
        pltpu.make_async_copy(wave_hbm.at[own_rows(f)], waves.at[0], lsems.at[2]),
    ]
    for copy in table_copies:
        copy.start()
    for step in range(TILES):
        v_copy(step, ids[step]).start()
    for part in range(4):
        u_copy(part).start()

    def targets(chunk, sign):
        return [shifted(me, chunk * GROUP + k, sign) for k in range(GROUP)]

    def transfer(phase, step):
        return pltpu.make_async_remote_copy(
            src_ref=send.at[phase, step], dst_ref=recv.at[phase, step],
            send_sem=ssem.at[phase, step], recv_sem=rsem.at[phase, step],
            device_id={"tile": shifted(me, step, 1)}, device_id_type=MESH,
        )

    def store(phase, chunk, values):
        for k in range(GROUP):
            send[phase, chunk * GROUP + k] = values[k]

        @pl.when(chunk == CHUNKS - 1)
        def _():
            recv[phase, last] = values[GROUP - 1]

    def depart(phase, chunk):
        for k in range(GROUP - 1):
            transfer(phase, chunk * GROUP + k).start()

        @pl.when(chunk < CHUNKS - 1)
        def _():
            transfer(phase, chunk * GROUP + GROUP - 1).start()

    def arrive(phase, chunk):
        for k in range(GROUP - 1):
            transfer(phase, chunk * GROUP + k).wait_recv()

        @pl.when(chunk < CHUNKS - 1)
        def _():
            transfer(phase, chunk * GROUP + GROUP - 1).wait_recv()

    def sent(phase):
        @pl.loop(0, last)
        def _(step):
            transfer(phase, step).wait_send()

    def contract(left, right):
        return lax.dot_general(
            left, right, (((0,), (0,)), ((), ())), preferred_element_type=F32
        )

    def code(half, chunk):
        ids = targets(chunk, 1)
        left = jnp.concatenate([vbuf[d, r] for d in ids for r in range(2)], 1)
        products = contract(left, xmat[half])
        values = []
        for k, d in enumerate(ids):
            at = 2 * k * WIDTH
            values.append(
                pack(
                    products[at : at + WIDTH], products[at + WIDTH : at + 2 * WIDTH],
                    rank_ref[me, 2 * d], rank_ref[me, 2 * d + 1],
                    scale_ref[me, 2 * d], scale_ref[me, 2 * d + 1],
                )
            )
        store(half, chunk, values)

    def loaded(chunk):
        for k in range(GROUP):
            v_copy(chunk * GROUP + k, 0).wait()

    def expand(half):
        acc[...] = jnp.zeros_like(acc)

        @pl.loop(0, CHUNKS)
        def _(chunk):
            arrive(half, chunk)
            ids = targets(chunk, -1)
            for k, j in enumerate(ids):
                first, second = unpack(
                    recv[half, chunk * GROUP + k],
                    rank_ref[j, 2 * me], rank_ref[j, 2 * me + 1],
                )
                dense[k * WIDTH : (k + 1) * WIDTH] = first
                dense[(GROUP + k) * WIDTH : (GROUP + k + 1) * WIDTH] = second
            for r in range(2):
                left = jnp.concatenate([ubuf[r, j] for j in ids], 1)
                right = dense[r * GROUP * WIDTH : (r + 1) * GROUP * WIDTH]
                acc[r] += jnp.dot(left, right, preferred_element_type=F32)

        for r in range(2):
            ybuf[half, r] = acc[r].astype(BF16)

    def code_back(half):
        @pl.loop(0, CHUNKS)
        def _(chunk):
            ids = targets(chunk, 1)
            products = [
                contract(
                    jnp.concatenate([ubuf[r, j] for j in ids], 1), ybuf[half, r]
                )
                for r in range(2)
            ]
            values = []
            for k, j in enumerate(ids):
                at = k * WIDTH
                values.append(
                    pack(
                        products[0][at : at + WIDTH], products[1][at : at + WIDTH],
                        rank_ref[j, 2 * me], rank_ref[j, 2 * me + 1],
                        scale_ref[j, 2 * me], scale_ref[j, 2 * me + 1],
                    )
                )
            store(2 + half, chunk, values)
            depart(2 + half, chunk)

    def expand_back(half):
        acc[0] = jnp.zeros((NB, NVS), F32)

        @pl.loop(0, CHUNKS)
        def _(chunk):
            arrive(2 + half, chunk)
            ids = targets(chunk, -1)
            for k, d in enumerate(ids):
                first, second = unpack(
                    recv[2 + half, chunk * GROUP + k],
                    rank_ref[me, 2 * d], rank_ref[me, 2 * d + 1],
                )
                dense[2 * k * WIDTH : (2 * k + 1) * WIDTH] = first
                dense[(2 * k + 1) * WIDTH : (2 * k + 2) * WIDTH] = second
            left = jnp.concatenate([vbuf[d, r] for d in ids for r in range(2)], 1)
            acc[0] += jnp.dot(left, dense[...], preferred_element_type=F32)

    def split(half):
        stripes[: 2 * NB] = waves[half].astype(F32)
        for p in range(2):
            part = stripes[pl.ds(p, NB, stride=2), :]
            xmat[half, :, p * HALF : (p + 1) * HALF] = part.astype(BF16)

    def merge(target):
        for p in range(2):
            stripes[pl.ds(p, NB, stride=2), :] = acc[0, :, p * HALF : (p + 1) * HALF]
        target[...] = stripes[: 2 * NB].astype(BF16)

    for copy in table_copies:
        copy.wait()
    split(0)
    loaded(0)
    code(0, 0)
    pl.semaphore_wait(barrier, TILES)
    depart(0, 0)
    x_copy = pltpu.make_async_remote_copy(
        src_ref=wave_hbm.at[own_rows(1 - f)], dst_ref=waves.at[1], send_sem=xsems.at[0],
        recv_sem=xsems.at[1], device_id=partner, device_id_type=MESH,
    )
    x_copy.start()

    @pl.loop(1, CHUNKS)
    def _(chunk):
        loaded(chunk)
        code(0, chunk)
        depart(0, chunk)

    x_copy.wait()
    split(1)

    @pl.loop(0, CHUNKS)
    def _(chunk):
        code(1, chunk)
        depart(1, chunk)

    for part in range(4):
        u_copy(part).wait()
    expand(0)
    code_back(0)
    expand(1)
    code_back(1)
    for r in range(2):
        for p in range(2):
            own = ybuf[0, r, :, p * HALF : (p + 1) * HALF].astype(F32)
            other = ybuf[1, r, :, p * HALF : (p + 1) * HALF].astype(F32)
            at = 4 * NB * r + p
            stripes[pl.ds(at, NB, stride=4), :] = jnp.where(f == 0, own, other)
            stripes[pl.ds(at + 2, NB, stride=4), :] = jnp.where(f == 0, other, own)
    fwd_ref[...] = stripes[...].astype(BF16)
    sent(0)
    sent(1)
    expand_back(0)
    merge(adj_ref.at[own_rows(f)])
    expand_back(1)
    merge(leaving)
    out_copy = pltpu.make_async_remote_copy(
        src_ref=leaving, dst_ref=adj_ref.at[own_rows(f)], send_sem=xsems.at[2],
        recv_sem=xsems.at[3], device_id=partner, device_id_type=MESH,
    )
    out_copy.start()
    sent(2)
    sent(3)
    out_copy.wait()


def hand_over(fwd_ref, adj_ref, fwd_hbm, adj_hbm, sems):
    copies = [
        pltpu.make_async_copy(fwd_ref, fwd_hbm, sems.at[0]),
        pltpu.make_async_copy(adj_ref, adj_hbm, sems.at[1]),
    ]
    for copy in copies:
        copy.start()
    for copy in copies:
        copy.wait()


def per_device(wave_in, column_basis, row_basis, tile_scale, tile_ranks):
    wave = wave_in.reshape(4 * NB, HALF)
    columns = column_basis.reshape(TILES, 2, NB, WIDTH)
    rows = row_basis.reshape(2, TILES, NB, WIDTH)
    anywhere = pl.BlockSpec(memory_space=pl.ANY)
    vmem = pl.BlockSpec(memory_space=pltpu.VMEM)
    packed = pltpu.VMEM((4, TILES, ROWS, HALF), BF16)
    forward, adjoint = pl.pallas_call(
        body,
        out_shape=(
            pltpu.VMEM((8 * NB, HALF), BF16),
            pltpu.VMEM((4 * NB, HALF), BF16),
        ),
        in_specs=[anywhere] * 5,
        out_specs=(vmem, vmem),
        scratch_shapes=[
            pltpu.SMEM((TILES, 2 * TILES), F32),
            pltpu.SMEM((TILES, 2 * TILES), jnp.int32),
            pltpu.VMEM((TILES, 2, NB, WIDTH), BF16),
            pltpu.VMEM((2, TILES, NB, WIDTH), BF16),
            pltpu.VMEM((2, 2 * NB, HALF), BF16),
            pltpu.VMEM((2, NB, NVS), BF16),
            pltpu.VMEM((2, 2, NB, NVS), BF16),
            packed, packed,
            pltpu.VMEM((2 * GROUP * WIDTH, NVS), BF16),
            pltpu.VMEM((2, NB, NVS), F32),
            pltpu.VMEM((8 * NB, HALF), F32),
            pltpu.VMEM((2 * NB, HALF), BF16),
            pltpu.SemaphoreType.DMA((TILES,)),
            pltpu.SemaphoreType.DMA((4,)),
            pltpu.SemaphoreType.DMA((4, TILES)),
            pltpu.SemaphoreType.DMA((4, TILES)),
            pltpu.SemaphoreType.DMA((4,)),
            pltpu.SemaphoreType.DMA((3,)),
        ],
        compiler_params=pltpu.CompilerParams(
            collective_id=0, has_side_effects=True, vmem_limit_bytes=56 << 20
        ),
        name="normal_operator",
    )(wave, columns, rows, tile_scale[0].T, tile_ranks[0].T)
    forward, adjoint = pl.pallas_call(
        hand_over,
        out_shape=(
            jax.ShapeDtypeStruct((8 * NB, HALF), BF16),
            jax.ShapeDtypeStruct((4 * NB, HALF), BF16),
        ),
        in_specs=[vmem, vmem],
        out_specs=(anywhere, anywhere),
        scratch_shapes=[pltpu.SemaphoreType.DMA((2,))],
        compiler_params=pltpu.CompilerParams(vmem_limit_bytes=4 << 20),
        name="hand_over",
    )(forward, adjoint)
    forward = forward.reshape(2 * NB, 2, 2, HALF).transpose(0, 2, 1, 3)
    forward_out = forward.reshape(1, 2 * NB, 2, NVS)
    adjoint_out = adjoint.reshape(2, NB, 2, HALF)
    return forward_out, adjoint_out


def solution(mesh):
    return jax.shard_map(
        per_device,
        mesh=mesh,
        in_specs=(
            P(None, "tile", None, "freq"),
            P("freq", None, "tile", None, None),
            P("freq", "tile", None, None, None),
            P("freq", None, None),
            P("freq", None, None),
        ),
        out_specs=(P("freq", "tile", None, None), P(None, "tile", None, "freq")),
        check_vma=False,
    )
```

```python
import functools
import jax
import jax.numpy as jnp
from jax import lax
from jax.experimental import pallas as pl
from jax.experimental.pallas import tpu as pltpu
from jax.sharding import PartitionSpec as P

NB = 256
RMAX = 64
NVS = 256
TILES = 64
HALF = NVS // 2
BLOCKS = RMAX // 16
WIDTH = 2 * RMAX
SLOTS = 5
ROWS = 32 * SLOTS
GROUP = 4
CHUNKS = TILES // GROUP
STRIDE = 27
MESH = pl.DeviceIdType.MESH
BF16 = jnp.bfloat16
F32 = jnp.float32


def offset_of(step):
    mixed = lax.rem((step + 1) * STRIDE, TILES)
    return mixed // 16, lax.rem(mixed // 4, 4), lax.rem(mixed, 4)


def shifted(me, step, sign):
    dy, dx, dz = offset_of(step)
    y, x, z = me // 16, lax.rem(me // 4, 4), lax.rem(me, 4)
    y = lax.rem(y + sign * dy + 4, 4)
    x = lax.rem(x + sign * dx + 4, 4)
    z = lax.rem(z + sign * dz + 4, 4)
    return (y * 4 + x) * 4 + z


def conj_block(products, block):
    top = products[32 * block : 32 * block + 16]
    low = products[32 * block + 16 : 32 * block + 32]
    real = top[:, :HALF] + low[:, HALF:]
    imag = top[:, HALF:] - low[:, :HALF]
    return jnp.concatenate([real, imag], 0)


def pack(products0, products1, rank0, rank1, scale0, scale1):
    slots = []
    for slot in range(SLOTS):
        value = None
        if slot < BLOCKS:
            weight = jnp.where(16 * slot < rank0, scale0, 0.0)
            value = conj_block(products0, slot) * weight
        if slot > 0:
            block = SLOTS - 1 - slot
            weight = jnp.where(16 * block < rank1, scale1, 0.0)
            other = conj_block(products1, block) * weight
            value = other if value is None else value + other
        slots.append(value.astype(BF16))
    return jnp.concatenate(slots, 0)


def unpack(packed, rank0, rank1):
    first, second = [], []
    for slot in range(SLOTS):
        real = packed[32 * slot : 32 * slot + 16]
        imag = packed[32 * slot + 16 : 32 * slot + 32]
        both = jnp.concatenate(
            [jnp.concatenate([real, imag], 1), jnp.concatenate([-imag, real], 1)], 0
        )
        if slot < BLOCKS:
            live = jnp.where(16 * slot < rank0, 1.0, 0.0).astype(BF16)
            first.append(both if slot == 0 else both * live)
        if slot > 0:
            block = SLOTS - 1 - slot
            live = jnp.where(16 * block < rank1, 1.0, 0.0).astype(BF16)
            second.append(both if block == 0 else both * live)
    return jnp.concatenate(first, 0), jnp.concatenate(second[::-1], 0)


def body(
    wave_hbm, col_hbm, row_hbm, scale_hbm, rank_hbm,
    fwd_ref, adj_ref,
    scale_ref, rank_ref, vbuf, ubuf, waves, xmat, ybuf, send, recv, dense, acc,
    stripes, leaving,
    vsem, usem, ssem, rsem, xsems, lsems,
):
    me = lax.axis_index("tile")
    f = lax.axis_index("freq")
    partner = {"freq": 1 - f}
    last = TILES - 1

    def v_copy(step, d):
        return pltpu.make_async_copy(col_hbm.at[d], vbuf.at[d], vsem.at[step])

    def u_copy(part):
        span = pl.ds(part * 16, 16)
        return pltpu.make_async_copy(
            row_hbm.at[:, span], ubuf.at[:, span], usem.at[part]
        )

    def own_rows(index):
        return pl.ds(pl.multiple_of(index * 2 * NB, 2 * NB), 2 * NB)

    barrier = pltpu.get_barrier_semaphore()
    ys = [16 * lax.rem(me // 16 + k, 4) for k in range(4)]
    xs = [4 * lax.rem(me // 4 + k, 4) for k in range(4)]
    zs = [lax.rem(me + k, 4) for k in range(4)]
    order = [(step + 1) * STRIDE % TILES for step in range(TILES)]
    ids = [ys[at // 16] + xs[at // 4 % 4] + zs[at % 4] for at in order]
    hops = [min(at // 16, 1) + min(at // 4 % 4, 1) + min(at % 4, 1)
            + (at // 16 == 2) + (at // 4 % 4 == 2) + (at % 4 == 2) for at in order]
    for step in sorted(range(last), key=lambda step: -hops[step]):
        pl.semaphore_signal(
            barrier, inc=1, device_id={"tile": ids[step]}, device_id_type=MESH
        )
    pl.semaphore_signal(barrier, inc=1, device_id=partner, device_id_type=MESH)
    table_copies = [
        pltpu.make_async_copy(scale_hbm, scale_ref, lsems.at[0]),
        pltpu.make_async_copy(rank_hbm, rank_ref, lsems.at[1]),
        pltpu.make_async_copy(wave_hbm.at[own_rows(f)], waves.at[0], lsems.at[2]),
    ]
    for copy in table_copies:
        copy.start()
    for step in range(TILES):
        v_copy(step, ids[step]).start()
    for part in range(4):
        u_copy(part).start()

    def targets(chunk, sign):
        return [shifted(me, chunk * GROUP + k, sign) for k in range(GROUP)]

    def transfer(phase, step):
        return pltpu.make_async_remote_copy(
            src_ref=send.at[phase, step], dst_ref=recv.at[phase, step],
            send_sem=ssem.at[phase, step], recv_sem=rsem.at[phase, step],
            device_id={"tile": shifted(me, step, 1)}, device_id_type=MESH,
        )

    def store(phase, chunk, values):
        for k in range(GROUP):
            send[phase, chunk * GROUP + k] = values[k]

        @pl.when(chunk == CHUNKS - 1)
        def _():
            recv[phase, last] = values[GROUP - 1]

    def depart(phase, chunk):
        for k in range(GROUP - 1):
            transfer(phase, chunk * GROUP + k).start()

        @pl.when(chunk < CHUNKS - 1)
        def _():
            transfer(phase, chunk * GROUP + GROUP - 1).start()

    def arrive(phase, chunk):
        for k in range(GROUP - 1):
            transfer(phase, chunk * GROUP + k).wait_recv()

        @pl.when(chunk < CHUNKS - 1)
        def _():
            transfer(phase, chunk * GROUP + GROUP - 1).wait_recv()

    def settle(phase, chunk):
        for k in range(GROUP - 1):
            transfer(phase, chunk * GROUP + k).wait_send()

        @pl.when(chunk < CHUNKS - 1)
        def _():
            transfer(phase, chunk * GROUP + GROUP - 1).wait_send()

    def sent(phase):
        @pl.loop(0, last)
        def _(step):
            transfer(phase, step).wait_send()

    def contract(left, right):
        return lax.dot_general(
            left, right, (((0,), (0,)), ((), ())), preferred_element_type=F32
        )

    def code(half, chunk):
        ids = targets(chunk, 1)
        left = jnp.concatenate([vbuf[d, r] for d in ids for r in range(2)], 1)
        products = contract(left, xmat[half])
        values = []
        for k, d in enumerate(ids):
            at = 2 * k * WIDTH
            values.append(
                pack(
                    products[at : at + WIDTH], products[at + WIDTH : at + 2 * WIDTH],
                    rank_ref[me, 2 * d], rank_ref[me, 2 * d + 1],
                    scale_ref[me, 2 * d], scale_ref[me, 2 * d + 1],
                )
            )
        store(half, chunk, values)

    def loaded(chunk):
        for k in range(GROUP):
            v_copy(chunk * GROUP + k, 0).wait()

    def expand(half):
        acc[...] = jnp.zeros_like(acc)

        @pl.loop(0, CHUNKS)
        def _(chunk):
            arrive(half, chunk)
            ids = targets(chunk, -1)
            for k, j in enumerate(ids):
                first, second = unpack(
                    recv[half, chunk * GROUP + k],
                    rank_ref[j, 2 * me], rank_ref[j, 2 * me + 1],
                )
                dense[k * WIDTH : (k + 1) * WIDTH] = first
                dense[(GROUP + k) * WIDTH : (GROUP + k + 1) * WIDTH] = second
            for r in range(2):
                left = jnp.concatenate([ubuf[r, j] for j in ids], 1)
                right = dense[r * GROUP * WIDTH : (r + 1) * GROUP * WIDTH]
                acc[r] += jnp.dot(left, right, preferred_element_type=F32)

        for r in range(2):
            ybuf[half, r] = acc[r].astype(BF16)

    def code_back(half):
        @pl.loop(0, CHUNKS)
        def _(chunk):
            ids = targets(chunk, 1)
            products = [
                contract(
                    jnp.concatenate([ubuf[r, j] for j in ids], 1), ybuf[half, r]
                )
                for r in range(2)
            ]
            values = []
            for k, j in enumerate(ids):
                at = k * WIDTH
                values.append(
                    pack(
                        products[0][at : at + WIDTH], products[1][at : at + WIDTH],
                        rank_ref[j, 2 * me], rank_ref[j, 2 * me + 1],
                        scale_ref[j, 2 * me], scale_ref[j, 2 * me + 1],
                    )
                )
            store(2 + half, chunk, values)
            depart(2 + half, chunk)

    def expand_back(half):
        @pl.loop(0, CHUNKS)
        def _(chunk):
            arrive(2 + half, chunk)
            ids = targets(chunk, -1)
            for k, d in enumerate(ids):
                first, second = unpack(
                    recv[2 + half, chunk * GROUP + k],
                    rank_ref[me, 2 * d], rank_ref[me, 2 * d + 1],
                )
                dense[2 * k * WIDTH : (2 * k + 1) * WIDTH] = first
                dense[(2 * k + 1) * WIDTH : (2 * k + 2) * WIDTH] = second
            left = jnp.concatenate([vbuf[d, r] for d in ids for r in range(2)], 1)
            acc[half] += jnp.dot(left, dense[...], preferred_element_type=F32)
            settle(2 + half, chunk)

    def split(half):
        stripes[: 2 * NB] = waves[half].astype(F32)
        for p in range(2):
            part = stripes[pl.ds(p, NB, stride=2), :]
            xmat[half, :, p * HALF : (p + 1) * HALF] = part.astype(BF16)

    def merge(half, target):
        for p in range(2):
            part = acc[half, :, p * HALF : (p + 1) * HALF]
            stripes[pl.ds(p, NB, stride=2), :] = part
        target[...] = stripes[: 2 * NB].astype(BF16)

    for copy in table_copies:
        copy.wait()
    split(0)
    loaded(0)
    code(0, 0)
    pl.semaphore_wait(barrier, TILES)
    depart(0, 0)
    x_copy = pltpu.make_async_remote_copy(
        src_ref=wave_hbm.at[own_rows(1 - f)], dst_ref=waves.at[1], send_sem=xsems.at[0],
        recv_sem=xsems.at[1], device_id=partner, device_id_type=MESH,
    )
    x_copy.start()

    @pl.loop(1, CHUNKS)
    def _(chunk):
        loaded(chunk)
        code(0, chunk)
        depart(0, chunk)

    x_copy.wait()
    split(1)

    @pl.loop(0, CHUNKS)
    def _(chunk):
        code(1, chunk)
        depart(1, chunk)

    for part in range(4):
        u_copy(part).wait()
    expand(0)
    code_back(0)
    expand(1)
    code_back(1)
    for r in range(2):
        for p in range(2):
            own = ybuf[0, r, :, p * HALF : (p + 1) * HALF].astype(F32)
            other = ybuf[1, r, :, p * HALF : (p + 1) * HALF].astype(F32)
            at = 4 * NB * r + p
            stripes[pl.ds(at, NB, stride=4), :] = jnp.where(f == 0, own, other)
            stripes[pl.ds(at + 2, NB, stride=4), :] = jnp.where(f == 0, other, own)
    fwd_ref[...] = stripes[...].astype(BF16)
    sent(0)
    sent(1)
    acc[...] = jnp.zeros_like(acc)
    expand_back(0)
    expand_back(1)
    merge(1, leaving)
    out_copy = pltpu.make_async_remote_copy(
        src_ref=leaving, dst_ref=adj_ref.at[own_rows(f)], send_sem=xsems.at[2],
        recv_sem=xsems.at[3], device_id=partner, device_id_type=MESH,
    )
    out_copy.start()
    merge(0, adj_ref.at[own_rows(f)])
    out_copy.wait()


def hand_over(fwd_ref, adj_ref, fwd_hbm, adj_hbm, sems):
    copies = [
        pltpu.make_async_copy(fwd_ref, fwd_hbm, sems.at[0]),
        pltpu.make_async_copy(adj_ref, adj_hbm, sems.at[1]),
    ]
    for copy in copies:
        copy.start()
    for copy in copies:
        copy.wait()


def per_device(wave_in, column_basis, row_basis, tile_scale, tile_ranks):
    wave = wave_in.reshape(4 * NB, HALF)
    columns = column_basis.reshape(TILES, 2, NB, WIDTH)
    rows = row_basis.reshape(2, TILES, NB, WIDTH)
    anywhere = pl.BlockSpec(memory_space=pl.ANY)
    vmem = pl.BlockSpec(memory_space=pltpu.VMEM)
    packed = pltpu.VMEM((4, TILES, ROWS, HALF), BF16)
    forward, adjoint = pl.pallas_call(
        body,
        out_shape=(
            pltpu.VMEM((8 * NB, HALF), BF16),
            pltpu.VMEM((4 * NB, HALF), BF16),
        ),
        in_specs=[anywhere] * 5,
        out_specs=(vmem, vmem),
        scratch_shapes=[
            pltpu.SMEM((TILES, 2 * TILES), F32),
            pltpu.SMEM((TILES, 2 * TILES), jnp.int32),
            pltpu.VMEM((TILES, 2, NB, WIDTH), BF16),
            pltpu.VMEM((2, TILES, NB, WIDTH), BF16),
            pltpu.VMEM((2, 2 * NB, HALF), BF16),
            pltpu.VMEM((2, NB, NVS), BF16),
            pltpu.VMEM((2, 2, NB, NVS), BF16),
            packed, packed,
            pltpu.VMEM((2 * GROUP * WIDTH, NVS), BF16),
            pltpu.VMEM((2, NB, NVS), F32),
            pltpu.VMEM((8 * NB, HALF), F32),
            pltpu.VMEM((2 * NB, HALF), BF16),
            pltpu.SemaphoreType.DMA((TILES,)),
            pltpu.SemaphoreType.DMA((4,)),
            pltpu.SemaphoreType.DMA((4, TILES)),
            pltpu.SemaphoreType.DMA((4, TILES)),
            pltpu.SemaphoreType.DMA((4,)),
            pltpu.SemaphoreType.DMA((3,)),
        ],
        compiler_params=pltpu.CompilerParams(
            collective_id=0, has_side_effects=True, vmem_limit_bytes=56 << 20
        ),
        name="normal_operator",
    )(wave, columns, rows, tile_scale[0].T, tile_ranks[0].T)
    forward, adjoint = pl.pallas_call(
        hand_over,
        out_shape=(
            jax.ShapeDtypeStruct((8 * NB, HALF), BF16),
            jax.ShapeDtypeStruct((4 * NB, HALF), BF16),
        ),
        in_specs=[vmem, vmem],
        out_specs=(anywhere, anywhere),
        scratch_shapes=[pltpu.SemaphoreType.DMA((2,))],
        compiler_params=pltpu.CompilerParams(vmem_limit_bytes=4 << 20),
        name="hand_over",
    )(forward, adjoint)
    forward = forward.reshape(2 * NB, 2, 2, HALF).transpose(0, 2, 1, 3)
    forward_out = forward.reshape(1, 2 * NB, 2, NVS)
    adjoint_out = adjoint.reshape(2, NB, 2, HALF)
    return forward_out, adjoint_out


def solution(mesh):
    return jax.shard_map(
        per_device,
        mesh=mesh,
        in_specs=(
            P(None, "tile", None, "freq"),
            P("freq", None, "tile", None, None),
            P("freq", "tile", None, None, None),
            P("freq", None, None),
            P("freq", None, None),
        ),
        out_specs=(P("freq", "tile", None, None), P(None, "tile", None, "freq")),
        check_vma=False,
    )
```

```python
import functools
import jax
import jax.numpy as jnp
from jax import lax
from jax.experimental import pallas as pl
from jax.experimental.pallas import tpu as pltpu
from jax.sharding import PartitionSpec as P

NB = 256
RMAX = 64
NVS = 256
TILES = 64
HALF = NVS // 2
BLOCKS = RMAX // 16
WIDTH = 2 * RMAX
SLOTS = 5
ROWS = 32 * SLOTS
GROUP = 4
CHUNKS = TILES // GROUP
STRIDE = 35
MESH = pl.DeviceIdType.MESH
BF16 = jnp.bfloat16
F32 = jnp.float32


def offset_of(step):
    mixed = lax.rem((step + 1) * STRIDE, TILES)
    return mixed // 16, lax.rem(mixed // 4, 4), lax.rem(mixed, 4)


def shifted(me, step, sign):
    dy, dx, dz = offset_of(step)
    y, x, z = me // 16, lax.rem(me // 4, 4), lax.rem(me, 4)
    y = lax.rem(y + sign * dy + 4, 4)
    x = lax.rem(x + sign * dx + 4, 4)
    z = lax.rem(z + sign * dz + 4, 4)
    return (y * 4 + x) * 4 + z


def conj_block(products, block):
    top = products[32 * block : 32 * block + 16]
    low = products[32 * block + 16 : 32 * block + 32]
    real = top[:, :HALF] + low[:, HALF:]
    imag = top[:, HALF:] - low[:, :HALF]
    return jnp.concatenate([real, imag], 0)


def pack(products0, products1, rank0, rank1, scale0, scale1):
    slots = []
    for slot in range(SLOTS):
        value = None
        if slot < BLOCKS:
            weight = jnp.where(16 * slot < rank0, scale0, 0.0)
            value = conj_block(products0, slot) * weight
        if slot > 0:
            block = SLOTS - 1 - slot
            weight = jnp.where(16 * block < rank1, scale1, 0.0)
            other = conj_block(products1, block) * weight
            value = other if value is None else value + other
        slots.append(value.astype(BF16))
    return jnp.concatenate(slots, 0)


def unpack(packed, rank0, rank1):
    first, second = [], []
    for slot in range(SLOTS):
        real = packed[32 * slot : 32 * slot + 16]
        imag = packed[32 * slot + 16 : 32 * slot + 32]
        both = jnp.concatenate(
            [jnp.concatenate([real, imag], 1), jnp.concatenate([-imag, real], 1)], 0
        )
        if slot < BLOCKS:
            live = jnp.where(16 * slot < rank0, 1.0, 0.0).astype(BF16)
            first.append(both if slot == 0 else both * live)
        if slot > 0:
            block = SLOTS - 1 - slot
            live = jnp.where(16 * block < rank1, 1.0, 0.0).astype(BF16)
            second.append(both if block == 0 else both * live)
    return jnp.concatenate(first, 0), jnp.concatenate(second[::-1], 0)


def body(
    wave_hbm, col_hbm, row_hbm, scale_hbm, rank_hbm,
    fwd_ref, adj_ref,
    scale_ref, rank_ref, vbuf, ubuf, waves, xmat, ybuf, send, recv, dense, acc,
    stripes, leaving,
    vsem, usem, ssem, rsem, xsems, lsems,
):
    me = lax.axis_index("tile")
    f = lax.axis_index("freq")
    partner = {"freq": 1 - f}
    last = TILES - 1

    def v_copy(step, d):
        return pltpu.make_async_copy(col_hbm.at[d], vbuf.at[d], vsem.at[step])

    def u_copy(part):
        span = pl.ds(part * 16, 16)
        return pltpu.make_async_copy(
            row_hbm.at[:, span], ubuf.at[:, span], usem.at[part]
        )

    def own_rows(index):
        return pl.ds(pl.multiple_of(index * 2 * NB, 2 * NB), 2 * NB)

    barrier = pltpu.get_barrier_semaphore()
    ys = [16 * lax.rem(me // 16 + k, 4) for k in range(4)]
    xs = [4 * lax.rem(me // 4 + k, 4) for k in range(4)]
    zs = [lax.rem(me + k, 4) for k in range(4)]
    order = [(step + 1) * STRIDE % TILES for step in range(TILES)]
    ids = [ys[at // 16] + xs[at // 4 % 4] + zs[at % 4] for at in order]
    hops = [min(at // 16, 1) + min(at // 4 % 4, 1) + min(at % 4, 1)
            + (at // 16 == 2) + (at // 4 % 4 == 2) + (at % 4 == 2) for at in order]
    for step in sorted(range(last), key=lambda step: -hops[step]):
        pl.semaphore_signal(
            barrier, inc=1, device_id={"tile": ids[step]}, device_id_type=MESH
        )
    pl.semaphore_signal(barrier, inc=1, device_id=partner, device_id_type=MESH)
    table_copies = [
        pltpu.make_async_copy(scale_hbm, scale_ref, lsems.at[0]),
        pltpu.make_async_copy(rank_hbm, rank_ref, lsems.at[1]),
        pltpu.make_async_copy(wave_hbm.at[own_rows(f)], waves.at[0], lsems.at[2]),
    ]
    for copy in table_copies:
        copy.start()
    for step in range(TILES):
        v_copy(step, ids[step]).start()
    for part in range(4):
        u_copy(part).start()

    def targets(chunk, sign):
        return [shifted(me, chunk * GROUP + k, sign) for k in range(GROUP)]

    def transfer(phase, step):
        return pltpu.make_async_remote_copy(
            src_ref=send.at[phase, step], dst_ref=recv.at[phase, step],
            send_sem=ssem.at[phase, step], recv_sem=rsem.at[phase, step],
            device_id={"tile": shifted(me, step, 1)}, device_id_type=MESH,
        )

    def store(phase, chunk, values):
        for k in range(GROUP):
            send[phase, chunk * GROUP + k] = values[k]

        @pl.when(chunk == CHUNKS - 1)
        def _():
            recv[phase, last] = values[GROUP - 1]

    def depart(phase, chunk):
        for k in range(GROUP - 1):
            transfer(phase, chunk * GROUP + k).start()

        @pl.when(chunk < CHUNKS - 1)
        def _():
            transfer(phase, chunk * GROUP + GROUP - 1).start()

    def arrive(phase, chunk):
        for k in range(GROUP - 1):
            transfer(phase, chunk * GROUP + k).wait_recv()

        @pl.when(chunk < CHUNKS - 1)
        def _():
            transfer(phase, chunk * GROUP + GROUP - 1).wait_recv()

    def settle(phase, chunk):
        for k in range(GROUP - 1):
            transfer(phase, chunk * GROUP + k).wait_send()

        @pl.when(chunk < CHUNKS - 1)
        def _():
            transfer(phase, chunk * GROUP + GROUP - 1).wait_send()

    def sent(phase):
        @pl.loop(0, last)
        def _(step):
            transfer(phase, step).wait_send()

    def contract(left, right):
        return lax.dot_general(
            left, right, (((0,), (0,)), ((), ())), preferred_element_type=F32
        )

    def code(half, chunk):
        ids = targets(chunk, 1)
        left = jnp.concatenate([vbuf[d, r] for d in ids for r in range(2)], 1)
        products = contract(left, xmat[half])
        values = []
        for k, d in enumerate(ids):
            at = 2 * k * WIDTH
            values.append(
                pack(
                    products[at : at + WIDTH], products[at + WIDTH : at + 2 * WIDTH],
                    rank_ref[me, 2 * d], rank_ref[me, 2 * d + 1],
                    scale_ref[me, 2 * d], scale_ref[me, 2 * d + 1],
                )
            )
        store(half, chunk, values)

    def loaded(chunk):
        for k in range(GROUP):
            v_copy(chunk * GROUP + k, 0).wait()

    def expand(half):
        acc[...] = jnp.zeros_like(acc)

        @pl.loop(0, CHUNKS)
        def _(chunk):
            arrive(half, chunk)
            ids = targets(chunk, -1)
            for k, j in enumerate(ids):
                first, second = unpack(
                    recv[half, chunk * GROUP + k],
                    rank_ref[j, 2 * me], rank_ref[j, 2 * me + 1],
                )
                dense[k * WIDTH : (k + 1) * WIDTH] = first
                dense[(GROUP + k) * WIDTH : (GROUP + k + 1) * WIDTH] = second
            for r in range(2):
                left = jnp.concatenate([ubuf[r, j] for j in ids], 1)
                right = dense[r * GROUP * WIDTH : (r + 1) * GROUP * WIDTH]
                acc[r] += jnp.dot(left, right, preferred_element_type=F32)

        for r in range(2):
            ybuf[half, r] = acc[r].astype(BF16)

    def code_back(half):
        @pl.loop(0, CHUNKS)
        def _(chunk):
            ids = targets(chunk, 1)
            products = [
                contract(
                    jnp.concatenate([ubuf[r, j] for j in ids], 1), ybuf[half, r]
                )
                for r in range(2)
            ]
            values = []
            for k, j in enumerate(ids):
                at = k * WIDTH
                values.append(
                    pack(
                        products[0][at : at + WIDTH], products[1][at : at + WIDTH],
                        rank_ref[j, 2 * me], rank_ref[j, 2 * me + 1],
                        scale_ref[j, 2 * me], scale_ref[j, 2 * me + 1],
                    )
                )
            store(2 + half, chunk, values)
            depart(2 + half, chunk)

    def expand_back(half):
        @pl.loop(0, CHUNKS)
        def _(chunk):
            arrive(2 + half, chunk)
            ids = targets(chunk, -1)
            for k, d in enumerate(ids):
                first, second = unpack(
                    recv[2 + half, chunk * GROUP + k],
                    rank_ref[me, 2 * d], rank_ref[me, 2 * d + 1],
                )
                dense[2 * k * WIDTH : (2 * k + 1) * WIDTH] = first
                dense[(2 * k + 1) * WIDTH : (2 * k + 2) * WIDTH] = second
            left = jnp.concatenate([vbuf[d, r] for d in ids for r in range(2)], 1)
            acc[half] += jnp.dot(left, dense[...], preferred_element_type=F32)
            settle(2 + half, chunk)

    def split(half):
        stripes[: 2 * NB] = waves[half].astype(F32)
        for p in range(2):
            part = stripes[pl.ds(p, NB, stride=2), :]
            xmat[half, :, p * HALF : (p + 1) * HALF] = part.astype(BF16)

    def merge(half, target):
        for p in range(2):
            part = acc[half, :, p * HALF : (p + 1) * HALF]
            stripes[pl.ds(p, NB, stride=2), :] = part
        target[...] = stripes[: 2 * NB].astype(BF16)

    for copy in table_copies:
        copy.wait()
    split(0)
    loaded(0)
    code(0, 0)
    pl.semaphore_wait(barrier, TILES)
    depart(0, 0)
    x_copy = pltpu.make_async_remote_copy(
        src_ref=wave_hbm.at[own_rows(1 - f)], dst_ref=waves.at[1], send_sem=xsems.at[0],
        recv_sem=xsems.at[1], device_id=partner, device_id_type=MESH,
    )
    x_copy.start()

    @pl.loop(1, CHUNKS)
    def _(chunk):
        loaded(chunk)
        code(0, chunk)
        depart(0, chunk)

    x_copy.wait()
    split(1)

    @pl.loop(0, CHUNKS)
    def _(chunk):
        code(1, chunk)
        depart(1, chunk)

    for part in range(4):
        u_copy(part).wait()
    expand(0)
    code_back(0)
    expand(1)
    code_back(1)
    for r in range(2):
        for p in range(2):
            own = ybuf[0, r, :, p * HALF : (p + 1) * HALF].astype(F32)
            other = ybuf[1, r, :, p * HALF : (p + 1) * HALF].astype(F32)
            at = 4 * NB * r + p
            stripes[pl.ds(at, NB, stride=4), :] = jnp.where(f == 0, own, other)
            stripes[pl.ds(at + 2, NB, stride=4), :] = jnp.where(f == 0, other, own)
    fwd_ref[...] = stripes[...].astype(BF16)
    sent(0)
    sent(1)
    acc[...] = jnp.zeros_like(acc)
    expand_back(0)
    expand_back(1)
    merge(1, leaving)
    out_copy = pltpu.make_async_remote_copy(
        src_ref=leaving, dst_ref=adj_ref.at[own_rows(f)], send_sem=xsems.at[2],
        recv_sem=xsems.at[3], device_id=partner, device_id_type=MESH,
    )
    out_copy.start()
    merge(0, adj_ref.at[own_rows(f)])
    out_copy.wait()


def hand_over(fwd_ref, adj_ref, fwd_hbm, adj_hbm, sems):
    copies = [
        pltpu.make_async_copy(fwd_ref, fwd_hbm, sems.at[0]),
        pltpu.make_async_copy(adj_ref, adj_hbm, sems.at[1]),
    ]
    for copy in copies:
        copy.start()
    for copy in copies:
        copy.wait()


def per_device(wave_in, column_basis, row_basis, tile_scale, tile_ranks):
    wave = wave_in.reshape(4 * NB, HALF)
    columns = column_basis.reshape(TILES, 2, NB, WIDTH)
    rows = row_basis.reshape(2, TILES, NB, WIDTH)
    anywhere = pl.BlockSpec(memory_space=pl.ANY)
    vmem = pl.BlockSpec(memory_space=pltpu.VMEM)
    packed = pltpu.VMEM((4, TILES, ROWS, HALF), BF16)
    forward, adjoint = pl.pallas_call(
        body,
        out_shape=(
            pltpu.VMEM((8 * NB, HALF), BF16),
            pltpu.VMEM((4 * NB, HALF), BF16),
        ),
        in_specs=[anywhere] * 5,
        out_specs=(vmem, vmem),
        scratch_shapes=[
            pltpu.SMEM((TILES, 2 * TILES), F32),
            pltpu.SMEM((TILES, 2 * TILES), jnp.int32),
            pltpu.VMEM((TILES, 2, NB, WIDTH), BF16),
            pltpu.VMEM((2, TILES, NB, WIDTH), BF16),
            pltpu.VMEM((2, 2 * NB, HALF), BF16),
            pltpu.VMEM((2, NB, NVS), BF16),
            pltpu.VMEM((2, 2, NB, NVS), BF16),
            packed, packed,
            pltpu.VMEM((2 * GROUP * WIDTH, NVS), BF16),
            pltpu.VMEM((2, NB, NVS), F32),
            pltpu.VMEM((8 * NB, HALF), F32),
            pltpu.VMEM((2 * NB, HALF), BF16),
            pltpu.SemaphoreType.DMA((TILES,)),
            pltpu.SemaphoreType.DMA((4,)),
            pltpu.SemaphoreType.DMA((4, TILES)),
            pltpu.SemaphoreType.DMA((4, TILES)),
            pltpu.SemaphoreType.DMA((4,)),
            pltpu.SemaphoreType.DMA((3,)),
        ],
        compiler_params=pltpu.CompilerParams(
            collective_id=0, has_side_effects=True, vmem_limit_bytes=56 << 20
        ),
        name="normal_operator",
    )(wave, columns, rows, tile_scale[0].T, tile_ranks[0].T)
    forward, adjoint = pl.pallas_call(
        hand_over,
        out_shape=(
            jax.ShapeDtypeStruct((8 * NB, HALF), BF16),
            jax.ShapeDtypeStruct((4 * NB, HALF), BF16),
        ),
        in_specs=[vmem, vmem],
        out_specs=(anywhere, anywhere),
        scratch_shapes=[pltpu.SemaphoreType.DMA((2,))],
        compiler_params=pltpu.CompilerParams(vmem_limit_bytes=4 << 20),
        name="hand_over",
    )(forward, adjoint)
    forward = forward.reshape(2 * NB, 2, 2, HALF).transpose(0, 2, 1, 3)
    forward_out = forward.reshape(1, 2 * NB, 2, NVS)
    adjoint_out = adjoint.reshape(2, NB, 2, HALF)
    return forward_out, adjoint_out


def solution(mesh):
    return jax.shard_map(
        per_device,
        mesh=mesh,
        in_specs=(
            P(None, "tile", None, "freq"),
            P("freq", None, "tile", None, None),
            P("freq", "tile", None, None, None),
            P("freq", None, None),
            P("freq", None, None),
        ),
        out_specs=(P("freq", "tile", None, None), P(None, "tile", None, "freq")),
        check_vma=False,
    )
```
